256 devices in a mesh: member: 4 (over y_hi, core), node: 64 (over y_lo, x, z).
Axes of the slice: x: 4, y: 4 (y_hi: 2, y_lo: 2; y = y_hi * 2 + y_lo), z: 8, core: 2. Of those that a mesh axis runs over, the one named last changes fastest.
Arguments:
- gridpoint_state: bfloat16 [218, 65536], P(None, 'node'), may hold values from -6 to 6
- grid_truth: bfloat16 [100, 65536], P(None, 'node'), may hold values from -6 to 6
- encoder_slots: int32 [16384, 16], P('node'), may hold values from 0 to 65535, as said below
- encoder_count: int32 [16384], P('node'), may hold values from 1 to 16
- node_reach: int32 [16384], P('node'), may hold values from 128 to 256
- decoder_slots: int32 [65536, 4], P('node'), may hold values from 0 to 16383, as said below
- member_perturb: bfloat16 [4, 16384, 1024], P('member', 'node'), may hold values from -6 to 6
- embed_weight: bfloat16 [218, 1024], replicated, may hold values from -0.4375 to 0.4375
- norm_gains: float32 [3, 1024], replicated, may hold values from 0.1 to 1.9
- qkv_weight: bfloat16 [1024, 3072], replicated
- out_weight: bfloat16 [1024, 1024], replicated, may hold values from -0.1875 to 0.1875
- up_weight: bfloat16 [1024, 4096], P('node'), may hold values from -0.1875 to 0.1875
- down_weight: bfloat16 [1024, 4096], P('node'), may hold values from -0.09375 to 0.09375
- head_weight: bfloat16 [1024, 100], replicated, may hold values from -0.1875 to 0.1875
Outputs:
- crps_grad: float32 [4, 100, 65536], P('member', None, 'node')
The draws below stay inside these ranges and needn't reach their ends.
Inputs may be any that keep to these rules, and one draw needn't show every extreme that they name: `encoder_slots`: for a hidden node of region r (nodes r * 256 to (r + 1) * 256 - 1), every slot names a grid point of region r - 1, r or r + 1, a region holding 1024 consecutive points; slots from encoder_count on are padding. `decoder_slots`: for a grid point of region r, every slot names a hidden node of region r - 1, r or r + 1.
All inputs are finite; a program needn't handle non-finite values.
Results may differ from the reference program's by a relative error of at most 0.0095.
The reference program's roundings to bfloat16 on the way count: a program that leaves them out, or rounds other values in their place, can miss the bound.
Values may be sent and summed in bfloat16 or wider, within the bound.
No kernel may reach another device: no remote copies, remote signals or barrier semaphores. Data moves between devices by JAX's collectives and lax.ppermute only.
A program may use at most 128 MiB of HBM per device.

```python
import jax
import jax.numpy as jnp
from jax import lax

D = 1024
HEADS = 16
HEAD_DIM = 64
FF = 4096
CH = 218
VARS = 100
BAND = 256
K_ENC = 16
K_DEC = 4
NODE_DEV = 256
GRID_DEV = 1024
NODES = 16384
POINTS = 65536
MEMBERS = 4


def window_slots(key, row_count, per_region, target_region, target_total, slot_count):
    region_count = target_total // target_region
    owners = jnp.arange(row_count, dtype=jnp.int32) // per_region
    lowest = jnp.maximum(owners - 1, 0) * target_region
    highest = jnp.minimum(owners + 2, region_count) * target_region
    drawn = jax.random.randint(key, (row_count, slot_count), 0, 3 * target_region, dtype=jnp.int32)
    return lowest[:, None] + drawn % (highest - lowest)[:, None]


def draw_encoder_slots(key, part):
    return window_slots(jax.random.fold_in(key, 11), NODES, NODE_DEV, GRID_DEV, POINTS, K_ENC)


def draw_decoder_slots(key, part):
    return window_slots(jax.random.fold_in(key, 23), POINTS, GRID_DEV, NODE_DEV, NODES, K_DEC)


def draw_qkv_weight(key, part):
    entries = jax.random.normal(jax.random.fold_in(key, 37), (D, 3 * D), jnp.float32) * D ** (-0.5)
    return entries.astype(jnp.bfloat16)


def touch_ends(array, rng, low, largest):
    spot = [jax.random.randint(jax.random.fold_in(rng, axis), (), 0, length) for axis, length in enumerate(array.shape)]
    widest = array.shape.index(max(array.shape))
    neighbour = spot[:widest] + [(spot[widest] + 1) % array.shape[widest]] + spot[widest + 1:]
    return array.at[tuple(spot)].set(low).at[tuple(neighbour)].set(largest)


def block_scale(own_key, shape, split, smallest, largest):
    def one(axis_at, shards_of):
        draws = jax.random.uniform(jax.random.fold_in(jax.random.fold_in(own_key, 6), axis_at), (shards_of,), jnp.float32, smallest / len(split), largest / len(split))
        return jnp.repeat(jnp.exp(draws), shape[axis_at] // shards_of).reshape((-1,) + (1,) * (len(shape) - axis_at - 1))

    factor_of = one(*split[0])
    for cut in split[1:]:
        factor_of = factor_of * one(*cut)
    return factor_of


def scatter_about(own_key, extent, deviation, reach, cuts=(), kind=jnp.bfloat16):
    values = deviation * jax.random.normal(own_key, extent, jnp.float32)
    if cuts:
        values = values * block_scale(own_key, extent, cuts, -0.22, 0.18)
    return jnp.clip(values, -reach, reach).astype(kind)


def setup_inputs(seed: int = 0) -> dict:
    keys = jax.random.split(jax.random.key(seed), 15)
    gridpoint_state = scatter_about(keys[0], (CH, POINTS), 1.0, 6.0, ((1, 64),))
    grid_truth = scatter_about(keys[1], (VARS, POINTS), 1.0, 6.0, ((1, 64),))
    encoder_slots = draw_encoder_slots(jax.random.fold_in(keys[14], 71), 0)
    encoder_count = touch_ends(jax.random.randint(keys[3], (NODES,), 1, K_ENC + 1), jax.random.fold_in(keys[3], 1), 1, K_ENC).astype(jnp.int32)
    node_reach = touch_ends(jax.random.randint(keys[4], (NODES,), BAND // 2, BAND + 1), jax.random.fold_in(keys[4], 1), BAND // 2, BAND).astype(jnp.int32)
    decoder_slots = draw_decoder_slots(jax.random.fold_in(keys[14], 71), 0)
    member_perturb = scatter_about(keys[6], (MEMBERS, NODES, D), 1.0, 6.0, ((0, 4), (1, 64)))
    embed_weight = scatter_about(keys[7], (CH, D), CH ** -0.5, 0.4375)
    norm_gains = jnp.clip(1.0 + 0.18 * jax.random.normal(keys[8], (3, D), jnp.float32), 0.1, 1.9)
    qkv_weight = draw_qkv_weight(jax.random.fold_in(keys[14], 71), 0)
    out_weight = scatter_about(keys[10], (D, D), D ** -0.5, 0.1875)
    up_weight = scatter_about(keys[11], (D, FF), D ** -0.5, 0.1875, ((0, 64),))
    down_weight = scatter_about(keys[12], (D, FF), FF ** -0.5, 0.09375, ((0, 64),))
    head_weight = scatter_about(keys[13], (D, VARS), D ** -0.5, 0.1875)
    return dict(gridpoint_state=gridpoint_state, grid_truth=grid_truth, encoder_slots=encoder_slots, encoder_count=encoder_count, node_reach=node_reach, decoder_slots=decoder_slots, member_perturb=member_perturb, embed_weight=embed_weight, norm_gains=norm_gains, qkv_weight=qkv_weight, out_weight=out_weight, up_weight=up_weight, down_weight=down_weight, head_weight=head_weight)


EPS = 1e-05
SMOOTH = 0.25

def layer_norm(entries, scale_gain):
    average = lax.optimization_barrier(jnp.mean(entries, axis=-1, keepdims=True))
    centred = entries - average
    variance = lax.optimization_barrier(jnp.mean(centred * centred, axis=-1, keepdims=True))
    return centred * lax.rsqrt(variance + EPS) * scale_gain

def score_gradient(difference):
    return difference * lax.rsqrt(difference * difference + SMOOTH * SMOOTH)

def banded_attention(query_rows, bordered, first_query, first_key, node_total, reaches):
    query_count = query_rows.shape[0]
    key_count = bordered.shape[0]
    model_width = query_rows.shape[1]
    key_heads = bordered[:, :model_width].reshape(key_count, HEADS, HEAD_DIM).astype(jnp.float32)
    value_heads = bordered[:, model_width:].reshape(key_count, HEADS, HEAD_DIM).astype(jnp.float32)
    queries = query_rows.reshape(query_count, HEADS, HEAD_DIM).astype(jnp.float32)
    scores = jnp.einsum('qhd,khd->hqk', queries, key_heads) * HEAD_DIM ** (-0.5)
    rows_at = first_query + jnp.arange(query_count, dtype=jnp.int32)
    cols_at = first_key + jnp.arange(key_count, dtype=jnp.int32)
    distance = jnp.abs(rows_at[:, None] - cols_at[None, :])
    allowed = (distance <= reaches[:, None]) & (cols_at[None, :] >= 0) & (cols_at[None, :] < node_total)
    masked = jnp.where(allowed[None], scores, -1e+30)
    highest = lax.optimization_barrier(jnp.max(masked, axis=-1, keepdims=True))
    weights = jnp.where(allowed[None], jnp.exp(masked - highest), 0.0)
    chances = (weights / lax.optimization_barrier(jnp.sum(weights, axis=-1, keepdims=True))).astype(jnp.bfloat16)
    blended = jnp.einsum('hqk,khd->qhd', chances.astype(jnp.float32), value_heads)
    return blended.reshape(query_count, model_width).astype(jnp.bfloat16)

def reference(gridpoint_state, grid_truth, encoder_slots, encoder_count, node_reach, decoder_slots, member_perturb, embed_weight, norm_gains, qkv_weight, out_weight, up_weight, down_weight, head_weight):
    columns = gridpoint_state.T
    used = (jnp.arange(K_ENC, dtype=jnp.int32)[None, :] < encoder_count[:, None]).astype(jnp.float32)
    pooled_sum = jnp.zeros((NODES, CH), jnp.float32)
    for position in range(K_ENC):
        picked = jnp.take(columns, encoder_slots[:, position], axis=0).astype(jnp.float32)
        pooled_sum = pooled_sum + picked * used[:, position:position + 1]
    pooled_nodes = (pooled_sum / encoder_count[:, None].astype(jnp.float32)).astype(jnp.bfloat16)
    embedded = jnp.dot(pooled_nodes, embed_weight, preferred_element_type=jnp.float32)
    head_wide = head_weight.astype(jnp.float32)

    def member_prediction(perturb_rows):
        hidden_start = embedded + perturb_rows.astype(jnp.float32)
        normed = layer_norm(hidden_start, norm_gains[0]).astype(jnp.bfloat16)
        project = jnp.dot(normed, qkv_weight, preferred_element_type=jnp.float32).astype(jnp.bfloat16)
        query_all = project[:, :D]
        padded = jnp.pad(project[:, D:], ((BAND, BAND), (0, 0)))

        def one_block(block):
            first = (block * NODE_DEV).astype(jnp.int32)
            query_rows = lax.dynamic_slice_in_dim(query_all, first, NODE_DEV, 0)
            bordered = lax.dynamic_slice_in_dim(padded, first, NODE_DEV + 2 * BAND, 0)
            reaches = lax.dynamic_slice_in_dim(node_reach, first, NODE_DEV, 0)
            return banded_attention(query_rows, bordered, first, first - BAND, NODES, reaches)
        attended = lax.map(one_block, jnp.arange(NODES // NODE_DEV, dtype=jnp.int32)).reshape(NODES, D)
        hidden_mid = hidden_start + jnp.dot(attended, out_weight, preferred_element_type=jnp.float32)
        normed_mid = layer_norm(hidden_mid, norm_gains[1]).astype(jnp.bfloat16)
        upper = jnp.dot(normed_mid, up_weight, preferred_element_type=jnp.float32)
        active = jax.nn.gelu(upper).astype(jnp.bfloat16)
        lowered = lax.dot_general(active, down_weight, (((1,), (1,)), ((), ())), preferred_element_type=jnp.float32)
        final = layer_norm(hidden_mid + lowered, norm_gains[2]).astype(jnp.bfloat16)
        summed = jnp.zeros((POINTS, D), jnp.float32)
        for position in range(K_DEC):
            summed = summed + jnp.take(final, decoder_slots[:, position], axis=0).astype(jnp.float32)
        gathered = summed / K_DEC
        state_delta = lax.dot_general(head_wide, gathered, (((0,), (1,)), ((), ())), precision=lax.Precision.HIGHEST, preferred_element_type=jnp.float32)
        return gridpoint_state[:VARS].astype(jnp.float32) + state_delta
    predicted_fields = lax.map(member_prediction, member_perturb)
    observed_field = grid_truth.astype(jnp.float32)
    gradients = []
    for member_index in range(MEMBERS):
        self_field = predicted_fields[member_index]
        pairwise_sum = jnp.zeros_like(self_field)
        for other_member in range(MEMBERS):
            pairwise_sum = pairwise_sum + score_gradient(self_field - predicted_fields[other_member])
        gradients.append(score_gradient(self_field - observed_field) / MEMBERS - pairwise_sum / (MEMBERS * (MEMBERS - 1)))
    return jnp.stack(gradients)
```

```python
import functools

import jax
import jax.numpy as jnp
from jax import lax
from jax.experimental import pallas as pl
from jax.experimental.pallas import tpu as pltpu
from jax.sharding import Mesh
from jax.sharding import PartitionSpec as P

HEADS = 16
HEAD_DIM = 64
BAND = 256
NODE = ("node_0", "node_1", "node_2")
MEMBER = ("member_hi", "member_core")

EPS = 1e-05
SMOOTH = 0.25

F32 = jnp.float32
BF16 = jnp.bfloat16
LANES_BOTH = (((1,), (1,)), ((), ()))


def params(mib):
    return pltpu.CompilerParams(vmem_limit_bytes=mib * 1024 * 1024)


def cost(flops, moved, transcendentals=0):
    return pl.CostEstimate(
        flops=int(flops), bytes_accessed=int(moved), transcendentals=int(transcendentals)
    )


def layer_norm(entries, scale_gain):
    average = jnp.mean(entries, axis=-1, keepdims=True)
    centred = entries - average
    variance = jnp.mean(centred * centred, axis=-1, keepdims=True)
    return centred * lax.rsqrt(variance + EPS) * scale_gain


def score_gradient(difference):
    return difference * lax.rsqrt(difference * difference + SMOOTH * SMOOTH)


def dot(left_side, right_side):
    return jnp.dot(left_side, right_side, preferred_element_type=F32)


def dot_lanes(left_side, right_side):
    return lax.dot_general(left_side, right_side, LANES_BOTH, preferred_element_type=F32)


def neighbours(block):
    count = lax.axis_size(NODE)
    forward = [(i, i + 1) for i in range(count - 1)]
    backward = [(target, source) for source, target in forward]
    return lax.ppermute(block, NODE, forward), lax.ppermute(block, NODE, backward)


def other_core(block):
    return lax.ppermute(block, "member_core", [(0, 1), (1, 0)])


def tally_kernel(slots_ref, out_ref):
    rows = 16
    width = out_ref.shape[1]
    chunk = 1024

    def body(step, carry):
        first = pl.multiple_of(step * rows, rows)
        slots = slots_ref[pl.ds(first, rows), :]
        for start in range(0, width, chunk):
            window = lax.broadcasted_iota(jnp.int32, (rows, chunk), 1) + start
            total = jnp.zeros((rows, chunk), F32)
            for position in range(slots.shape[1]):
                hit = slots[:, position : position + 1] == window
                total = total + jnp.where(hit, 1.0, 0.0)
            out_ref[pl.ds(first, rows), start : start + chunk] = total.astype(BF16)
        return carry

    lax.fori_loop(0, out_ref.shape[0] // rows, body, 0)


def encoder_tallies(slots, width):
    nodes, count = slots.shape
    return pl.pallas_call(
        tally_kernel,
        out_shape=jax.ShapeDtypeStruct((nodes, width), BF16),
        compiler_params=params(16),
        cost_estimate=cost(3 * nodes * width * count, nodes * width * 2),
        name="encoder_tallies",
    )(slots)


def pooled_kernel(tally_ref, low_ref, own_ref, high_ref, count_ref, out_ref):
    width = low_ref.shape[1]
    total = dot_lanes(tally_ref[:, width : 2 * width], own_ref[...])
    total = total + dot_lanes(tally_ref[:, :width], low_ref[...])
    total = total + dot_lanes(tally_ref[:, 2 * width :], high_ref[...])
    out_ref[...] = (total / count_ref[...]).astype(BF16)


def pool(tallies, low, own, high, counts):
    nodes = tallies.shape[0]
    channels = own.shape[0]
    return pl.pallas_call(
        pooled_kernel,
        out_shape=jax.ShapeDtypeStruct((nodes, channels), BF16),
        compiler_params=params(24),
        cost_estimate=cost(2 * nodes * tallies.shape[1] * channels, tallies.size * 4),
        name="pooled",
    )(tallies, low, own, high, counts)


def qkv_kernel(
    pool_low, pool_own, pool_high, per_low, per_own, per_high, embed_ref, gain_ref, qkv_hbm,
    start_ref, query_ref, kv_ref, qkv_ref, sem,
):
    copy = pltpu.make_async_copy(qkv_hbm, qkv_ref, sem)
    copy.start()
    nodes, width = start_ref.shape
    gain = gain_ref[0:1, :]

    def start_of(pooled, perturb):
        return dot(pooled[...], embed_ref[...]) + perturb[...].astype(F32)

    normed = []
    for place, (pooled, perturb) in enumerate(
        ((pool_low, per_low), (pool_own, per_own), (pool_high, per_high))
    ):
        start = start_of(pooled, perturb)
        if place == 1:
            start_ref[...] = start
        normed.append(layer_norm(start, gain).astype(BF16))
    copy.wait()
    query = dot(normed[1], qkv_ref[:, :width]).astype(BF16)
    query_ref[...] = query * jnp.asarray(HEAD_DIM ** (-0.5), BF16)
    for place in range(3):
        for half in range(2):
            columns = slice((half + 1) * width, (half + 2) * width)
            kv_ref[place * nodes : (place + 1) * nodes, half * width : (half + 1) * width] = dot(
                normed[place], qkv_ref[:, columns]
            ).astype(BF16)


def qkv(pooled, perturbs, embed_weight, norm_gains, qkv_weight):
    nodes, width = perturbs[1].shape
    vmem = pl.BlockSpec(memory_space=pltpu.VMEM)
    return pl.pallas_call(
        qkv_kernel,
        out_shape=(
            jax.ShapeDtypeStruct((nodes, width), F32),
            jax.ShapeDtypeStruct((nodes, width), BF16),
            jax.ShapeDtypeStruct((3 * nodes, 2 * width), BF16),
        ),
        in_specs=[vmem] * 8 + [pl.BlockSpec(memory_space=pl.ANY)],
        scratch_shapes=[pltpu.VMEM(qkv_weight.shape, BF16), pltpu.SemaphoreType.DMA],
        compiler_params=params(44),
        cost_estimate=cost(2 * 7 * nodes * width * width, 16 << 20),
        name="embed_qkv",
    )(*pooled, *perturbs, embed_weight, norm_gains, qkv_weight)


def attention_kernel(
    where_ref, query_ref, kv_ref, reach_ref, start_ref, gain_ref, out_hbm,
    mid_ref, normed_ref, cap_ref, attended_ref, out_ref, sem,
):
    copy = pltpu.make_async_copy(out_hbm, out_ref, sem)
    copy.start()
    nodes, width = query_ref.shape
    rows = cap_ref.shape[1]
    span = cap_ref.shape[2]
    first_query = where_ref[0]
    node_total = where_ref[1]
    for block in range(nodes // rows):
        at = first_query + block * rows + lax.broadcasted_iota(jnp.int32, (rows, span), 0)
        key = first_query - BAND + block * rows + lax.broadcasted_iota(jnp.int32, (rows, span), 1)
        reach = reach_ref[block * rows : (block + 1) * rows, :]
        allowed = (jnp.abs(at - key) <= reach) & (key >= 0) & (key < node_total)
        cap_ref[block] = jnp.where(allowed, 3e38, -1e30)

    lane = lax.broadcasted_iota(jnp.int32, (1, 2 * HEAD_DIM), 1)
    for block in range(nodes // rows):
        cap = cap_ref.at[block]
        for pair in range(HEADS // 2):
            columns = slice(pair * 2 * HEAD_DIM, (pair + 1) * 2 * HEAD_DIM)
            value_columns = slice(width + pair * 2 * HEAD_DIM, width + (pair + 1) * 2 * HEAD_DIM)
            queries = query_ref[block * rows : (block + 1) * rows, columns]
            keys = kv_ref[block * rows : block * rows + span, columns]
            values = kv_ref[block * rows : block * rows + span, value_columns]
            halves = []
            for side in range(2):
                mine = (lane < HEAD_DIM) if side == 0 else (lane >= HEAD_DIM)
                chosen = jnp.where(mine, queries, jnp.zeros_like(queries))
                scores = jnp.minimum(dot_lanes(chosen, keys), cap[...])
                highest = jnp.max(scores, axis=-1, keepdims=True)
                weights = jnp.exp(scores - highest)
                total = jnp.sum(weights, axis=-1, keepdims=True)
                blended = dot(weights.astype(BF16), values)
                halves.append(blended * (1.0 / total))
            attended_ref[block * rows : (block + 1) * rows, columns] = jnp.where(
                lane < HEAD_DIM, halves[0], halves[1]
            ).astype(BF16)
    copy.wait()
    middle = start_ref[...] + dot(attended_ref[...], out_ref[...])
    mid_ref[...] = middle
    normed_ref[...] = layer_norm(middle, gain_ref[1:2, :]).astype(BF16)


def attention(where, query, kv, reach, start, norm_gains, out_weight):
    nodes, width = query.shape
    rows = 128
    span = rows + 2 * BAND
    vmem = pl.BlockSpec(memory_space=pltpu.VMEM)
    return pl.pallas_call(
        attention_kernel,
        out_shape=(
            jax.ShapeDtypeStruct((nodes, width), F32),
            jax.ShapeDtypeStruct((nodes, width), BF16),
        ),
        in_specs=[pl.BlockSpec(memory_space=pltpu.SMEM)]
        + [vmem] * 5
        + [pl.BlockSpec(memory_space=pl.ANY)],
        scratch_shapes=[
            pltpu.VMEM((nodes // rows, rows, span), F32),
            pltpu.VMEM((nodes, width), BF16),
            pltpu.VMEM(out_weight.shape, BF16),
            pltpu.SemaphoreType.DMA,
        ],
        compiler_params=params(32),
        cost_estimate=cost(
            4 * nodes * span * width + 2 * nodes * width * width,
            10 << 20,
            nodes * span * HEADS,
        ),
        name="attention",
    )(where, query, kv, reach, start, norm_gains, out_weight)


def mlp_kernel(tokens_ref, weight_ref, out_ref):
    blocks, sides, rows, columns = weight_ref.shape
    rows = rows // 2
    part = blocks * rows

    upper = None
    for side in range(sides):
        up = weight_ref[:, side, :rows, :].reshape(part, columns)
        term = dot(tokens_ref[:, side * part : (side + 1) * part], up)
        upper = term if upper is None else upper + term
    active = jax.nn.gelu(upper).astype(BF16)
    lowered = []
    for side in range(sides):
        down = weight_ref[:, side, rows:, :].reshape(part, columns)
        lowered.append(dot_lanes(active, down))

    @pl.when(pl.program_id(0) == 0)
    def _():
        for side in range(sides):
            out_ref[:, side * part : (side + 1) * part] = lowered[side]

    @pl.when(pl.program_id(0) > 0)
    def _():
        for side in range(sides):
            out_ref[:, side * part : (side + 1) * part] += lowered[side]


def mlp_part(tokens, weights):
    nodes, width = tokens.shape
    blocks, sides, rows, hidden = weights.shape
    step = 512
    return pl.pallas_call(
        mlp_kernel,
        grid=(hidden // step,),
        out_shape=jax.ShapeDtypeStruct((nodes, width), F32),
        in_specs=[
            pl.BlockSpec((nodes, width), lambda j: (0, 0)),
            pl.BlockSpec((blocks, sides, rows, step), lambda j: (0, 0, 0, j)),
        ],
        out_specs=pl.BlockSpec((nodes, width), lambda j: (0, 0)),
        compiler_params=params(32),
        cost_estimate=cost(4 * nodes * width * hidden, weights.size * 2, nodes * hidden),
        name="mlp_part",
    )(tokens, weights)


def head_kernel(mid_ref, own_ref, other_ref, gain_ref, head_ref, out_ref):
    ending = mid_ref[...] + (own_ref[...] + other_ref[...])
    final = layer_norm(ending, gain_ref[2:3, :]).astype(BF16)
    out_ref[...] = dot_lanes(head_ref[...], final).astype(BF16)


def head(middle, own, other, norm_gains, head_rows):
    nodes, width = middle.shape
    variables = head_rows.shape[0]
    return pl.pallas_call(
        head_kernel,
        out_shape=jax.ShapeDtypeStruct((variables, nodes), BF16),
        compiler_params=params(24),
        cost_estimate=cost(2 * nodes * width * variables, 4 << 20),
        name="final_head",
    )(middle, own, other, norm_gains, head_rows)


def decoder_tally_kernel(slots_ref, out_ref):
    rows = 64
    points = out_ref.shape[1]
    slots = slots_ref.shape[0]

    def body(step, carry):
        first = pl.multiple_of(step * rows, rows)
        node = first + lax.broadcasted_iota(jnp.int32, (rows, points), 0)
        total = jnp.zeros((rows, points), F32)
        for position in range(slots):
            hit = slots_ref[position : position + 1, :] == node
            total = total + jnp.where(hit, 1.0 / slots, 0.0)
        out_ref[pl.ds(first, rows), :] = total.astype(BF16)
        return carry

    lax.fori_loop(0, out_ref.shape[0] // rows, body, 0)


def decoder_tallies(slots, nodes):
    count, points = slots.shape
    return pl.pallas_call(
        decoder_tally_kernel,
        out_shape=jax.ShapeDtypeStruct((nodes, points), BF16),
        compiler_params=params(16),
        cost_estimate=cost(3 * nodes * points * count, nodes * points * 2),
        name="decoder_tallies",
    )(slots)


def crps_kernel(tally_ref, state_ref, truth_ref, *refs):
    out_ref = refs[-1]
    refs = refs[:-1]
    variables = out_ref.shape[0]
    nodes = refs[0].shape[1]
    state = state_ref[:variables, :].astype(F32)
    forecasts = []
    for member in range(len(refs) // 3):
        field = None
        for place in range(3):
            term = dot(
                refs[3 * member + place][...], tally_ref[place * nodes : (place + 1) * nodes, :]
            )
            field = term if field is None else field + term
        forecasts.append(state + field)
    members = len(forecasts)
    own = forecasts[0]
    pairwise = None
    for other in forecasts:
        term = score_gradient(own - other)
        pairwise = term if pairwise is None else pairwise + term
    out_ref[...] = score_gradient(own - truth_ref[...].astype(F32)) * (
        1.0 / members
    ) - pairwise * (1.0 / (members * (members - 1)))


def crps(tallies, state, truth, projected):
    variables, points = truth.shape
    return pl.pallas_call(
        crps_kernel,
        out_shape=jax.ShapeDtypeStruct((variables, points), F32),
        compiler_params=params(32),
        cost_estimate=cost(2 * 4 * variables * points * tallies.shape[0], 4 << 20),
        name="decoder_crps",
    )(tallies, state, truth, *projected)


def per_device(
    gridpoint_state,
    grid_truth,
    encoder_slots,
    encoder_count,
    node_reach,
    decoder_slots,
    member_perturb,
    embed_weight,
    norm_gains,
    qkv_weight,
    out_weight,
    up_weight,
    down_weight,
    head_weight,
):
    region = lax.axis_index(NODE)
    region_count = lax.axis_size(NODE)
    core = lax.axis_index("member_core")
    grid_dev = gridpoint_state.shape[1]
    node_dev = encoder_slots.shape[0]
    hidden = up_weight.shape[1] // 2
    perturb = member_perturb[0]

    share = jnp.concatenate(
        [
            lax.dynamic_slice_in_dim(up_weight, core * hidden, hidden, 1),
            lax.dynamic_slice_in_dim(down_weight, core * hidden, hidden, 1),
        ],
        axis=0,
    )
    pair = lax.all_gather(share, NODE[0], axis=0)
    weights = lax.all_gather(pair, NODE[1:], axis=0)

    state_low, state_high = neighbours(gridpoint_state)
    perturb_low, perturb_high = neighbours(perturb)

    positions = jnp.arange(encoder_slots.shape[1], dtype=jnp.int32)
    local_slots = jnp.where(
        positions[None, :] < encoder_count[:, None],
        encoder_slots - (region - 1) * grid_dev,
        -1,
    )
    tallies = encoder_tallies(local_slots, 3 * grid_dev)
    near_slots = (decoder_slots - (region - 1) * node_dev).T
    decoder_near = decoder_tallies(near_slots, 3 * node_dev)
    counts = encoder_count[:, None].astype(F32)
    pooled = pool(tallies, state_low, gridpoint_state, state_high, counts)
    pooled_low, pooled_high = neighbours(pooled)
    start, query, kv = qkv(
        (pooled_low, pooled, pooled_high),
        (perturb_low, perturb, perturb_high),
        embed_weight,
        norm_gains,
        qkv_weight,
    )
    where = jnp.stack([region * node_dev, jnp.int32(region_count * node_dev)])
    middle, normed_mid = attention(
        where, query, kv, node_reach[:, None], start, norm_gains, out_weight
    )

    normed_other = other_core(normed_mid)
    part_other = mlp_part(normed_other, weights)
    part_mine = mlp_part(normed_mid, weights)
    projected = head(middle, part_mine, other_core(part_other), norm_gains, head_weight.T)

    both = jnp.stack([projected, other_core(projected)])
    axes = ("member_hi",) + NODE
    def sent(step, flip):
        links = []
        for side in range(2):
            for i in range(region_count):
                j = i + step
                if 0 <= j < region_count:
                    target = (1 - side) if flip else side
                    links.append((side * region_count + i, target * region_count + j))
        return lax.ppermute(both, axes, links)

    low, high = sent(1, False), sent(-1, False)
    far_low, far_own, far_high = sent(1, True), sent(0, True), sent(-1, True)
    projected_all = []
    for near in ((low, both, high), (far_low, far_own, far_high)):
        for k in range(2):
            projected_all += [block[k] for block in near]
    gradient = crps(decoder_near, gridpoint_state, grid_truth, projected_all)
    return gradient[None]


def solution(mesh):
    torus = Mesh(
        mesh.devices.reshape(2, 2, 2, 4, 8),
        MEMBER + NODE,
    )
    return jax.shard_map(
        per_device,
        mesh=torus,
        in_specs=(
            P(None, NODE),
            P(None, NODE),
            P(NODE, None),
            P(NODE),
            P(NODE),
            P(NODE, None),
            P(MEMBER, NODE, None),
            P(),
            P(),
            P(),
            P(),
            P(NODE, None),
            P(NODE, None),
            P(),
        ),
        out_specs=P(MEMBER, None, NODE),
        check_vma=False,
    )
```

```python
import jax
import jax.numpy as jnp
from jax import lax
from jax.experimental import pallas as pl
from jax.experimental.pallas import tpu as pltpu
from jax.sharding import Mesh
from jax.sharding import PartitionSpec as P

HEADS = 16
HEAD_DIM = 64
BAND = 256
NODE = ("node_0", "node_1", "node_2")
MEMBER = ("member_hi", "member_core")

EPS = 1e-05
SMOOTH = 0.25

F32 = jnp.float32
BF16 = jnp.bfloat16
LANES_BOTH = (((1,), (1,)), ((), ()))


def params(mib):
    return pltpu.CompilerParams(vmem_limit_bytes=mib * 1024 * 1024)


def cost(flops, moved, transcendentals=0):
    return pl.CostEstimate(
        flops=int(flops), bytes_accessed=int(moved), transcendentals=int(transcendentals)
    )


def layer_norm(entries, scale_gain):
    average = jnp.mean(entries, axis=-1, keepdims=True)
    centred = entries - average
    variance = jnp.mean(centred * centred, axis=-1, keepdims=True)
    return centred * lax.rsqrt(variance + EPS) * scale_gain


def score_gradient(difference):
    return difference * lax.rsqrt(difference * difference + SMOOTH * SMOOTH)


def dot(left_side, right_side):
    return jnp.dot(left_side, right_side, preferred_element_type=F32)


def dot_lanes(left_side, right_side):
    return lax.dot_general(left_side, right_side, LANES_BOTH, preferred_element_type=F32)


def neighbours(block):
    count = lax.axis_size(NODE)
    forward = [(i, i + 1) for i in range(count - 1)]
    backward = [(target, source) for source, target in forward]
    return lax.ppermute(block, NODE, forward), lax.ppermute(block, NODE, backward)


def other_core(block):
    return lax.ppermute(block, "member_core", [(0, 1), (1, 0)])


def tally_kernel(place_ref, slots_ref, count_ref, out_ref):
    rows = 64
    nodes = out_ref.shape[1]
    slots = slots_ref[...] - place_ref[2]
    used = lax.broadcasted_iota(jnp.int32, slots.shape, 0) < count_ref[...]
    slots = jnp.where(used, slots, -1)

    def body(step, carry):
        first = pl.multiple_of(step * rows, rows)
        window = first + lax.broadcasted_iota(jnp.int32, (rows, nodes), 0)
        total = jnp.zeros((rows, nodes), F32)
        for position in range(slots.shape[0]):
            hit = slots[position : position + 1, :] == window
            total = total + jnp.where(hit, 1.0, 0.0)
        out_ref[pl.ds(first, rows), :] = total.astype(BF16)
        return carry

    lax.fori_loop(0, out_ref.shape[0] // rows, body, 0)


def encoder_tallies(place, slots, counts, width):
    count, nodes = slots.shape
    vmem = pl.BlockSpec(memory_space=pltpu.VMEM)
    return pl.pallas_call(
        tally_kernel,
        out_shape=jax.ShapeDtypeStruct((width, nodes), BF16),
        in_specs=[pl.BlockSpec(memory_space=pltpu.SMEM), vmem, vmem],
        compiler_params=params(16),
        cost_estimate=cost(3 * nodes * width * count, nodes * width * 2),
        name="encoder_tallies",
    )(place, slots, counts)


def pooled_kernel(tally_ref, low_ref, own_ref, high_ref, count_ref, out_ref):
    width = low_ref.shape[1]
    total = dot(own_ref[...], tally_ref[width : 2 * width, :])
    total = total + dot(low_ref[...], tally_ref[:width, :])
    total = total + dot(high_ref[...], tally_ref[2 * width :, :])
    out_ref[...] = (total / count_ref[...].astype(F32)).astype(BF16)


def pool(tallies, low, own, high, counts):
    nodes = tallies.shape[1]
    channels = own.shape[0]
    return pl.pallas_call(
        pooled_kernel,
        out_shape=jax.ShapeDtypeStruct((channels, nodes), BF16),
        compiler_params=params(24),
        cost_estimate=cost(2 * tallies.size * channels, tallies.size * 4),
        name="pooled",
    )(tallies, low, own, high, counts)


def qkv_kernel(
    pool_low, pool_own, pool_high, per_low, per_own, per_high, embed_ref, gain_ref, qkv_hbm,
    start_ref, query_ref, kv_ref, qkv_ref, sem,
):
    copy = pltpu.make_async_copy(qkv_hbm, qkv_ref, sem)
    copy.start()
    nodes, width = start_ref.shape
    gain = gain_ref[0:1, :]

    def start_of(pooled, perturb):
        embedded = lax.dot_general(
            pooled[...], embed_ref[...], (((0,), (0,)), ((), ())), preferred_element_type=F32
        )
        return embedded + perturb[...].astype(F32)

    normed = []
    for place, (pooled, perturb) in enumerate(
        ((pool_low, per_low), (pool_own, per_own), (pool_high, per_high))
    ):
        start = start_of(pooled, perturb)
        if place == 1:
            start_ref[...] = start
        normed.append(layer_norm(start, gain).astype(BF16))
    copy.wait()
    query = dot(normed[1], qkv_ref[:, :width]).astype(BF16)
    query_ref[...] = query * jnp.asarray(HEAD_DIM ** (-0.5), BF16)
    for place in range(3):
        for half in range(2):
            columns = slice((half + 1) * width, (half + 2) * width)
            kv_ref[place * nodes : (place + 1) * nodes, half * width : (half + 1) * width] = dot(
                normed[place], qkv_ref[:, columns]
            ).astype(BF16)


def qkv(pooled, perturbs, embed_weight, norm_gains, qkv_weight):
    nodes, width = perturbs[1].shape
    vmem = pl.BlockSpec(memory_space=pltpu.VMEM)
    return pl.pallas_call(
        qkv_kernel,
        out_shape=(
            jax.ShapeDtypeStruct((nodes, width), F32),
            jax.ShapeDtypeStruct((nodes, width), BF16),
            jax.ShapeDtypeStruct((3 * nodes, 2 * width), BF16),
        ),
        in_specs=[vmem] * 8 + [pl.BlockSpec(memory_space=pl.ANY)],
        scratch_shapes=[pltpu.VMEM(qkv_weight.shape, BF16), pltpu.SemaphoreType.DMA],
        compiler_params=params(44),
        cost_estimate=cost(2 * 7 * nodes * width * width, 16 << 20),
        name="embed_qkv",
    )(*pooled, *perturbs, embed_weight, norm_gains, qkv_weight)


def attention_kernel(
    where_ref, query_ref, kv_ref, reach_ref, start_ref, gain_ref, out_hbm,
    mid_ref, normed_ref, cap_ref, attended_ref, out_ref, sem,
):
    copy = pltpu.make_async_copy(out_hbm, out_ref, sem)
    copy.start()
    nodes, width = query_ref.shape
    rows = cap_ref.shape[1]
    span = cap_ref.shape[2]
    first_query = where_ref[0]
    node_total = where_ref[1]
    reaches = jnp.transpose(jnp.broadcast_to(reach_ref[...].astype(F32), (128, nodes)))
    for block in range(nodes // rows):
        at = first_query + block * rows + lax.broadcasted_iota(jnp.int32, (rows, span), 0)
        key = first_query - BAND + block * rows + lax.broadcasted_iota(jnp.int32, (rows, span), 1)
        reach = reaches[block * rows : (block + 1) * rows, :1].astype(jnp.int32)
        allowed = (jnp.abs(at - key) <= reach) & (key >= 0) & (key < node_total)
        cap_ref[block] = jnp.where(allowed, 3e38, -1e30)

    lane = lax.broadcasted_iota(jnp.int32, (1, 2 * HEAD_DIM), 1)
    for block in range(nodes // rows):
        cap = cap_ref.at[block]
        for pair in range(HEADS // 2):
            columns = slice(pair * 2 * HEAD_DIM, (pair + 1) * 2 * HEAD_DIM)
            value_columns = slice(width + pair * 2 * HEAD_DIM, width + (pair + 1) * 2 * HEAD_DIM)
            queries = query_ref[block * rows : (block + 1) * rows, columns]
            keys = kv_ref[block * rows : block * rows + span, columns]
            values = kv_ref[block * rows : block * rows + span, value_columns]
            halves = []
            for side in range(2):
                mine = (lane < HEAD_DIM) if side == 0 else (lane >= HEAD_DIM)
                chosen = jnp.where(mine, queries, jnp.zeros_like(queries))
                scores = jnp.minimum(dot_lanes(chosen, keys), cap[...])
                highest = jnp.max(scores, axis=-1, keepdims=True)
                weights = jnp.exp(scores - highest)
                total = jnp.sum(weights, axis=-1, keepdims=True)
                blended = dot(weights.astype(BF16), values)
                halves.append(blended * (1.0 / total))
            attended_ref[block * rows : (block + 1) * rows, columns] = jnp.where(
                lane < HEAD_DIM, halves[0], halves[1]
            ).astype(BF16)
    copy.wait()
    middle = start_ref[...] + dot(attended_ref[...], out_ref[...])
    mid_ref[...] = middle
    normed_ref[...] = layer_norm(middle, gain_ref[1:2, :]).astype(BF16)


def attention(where, query, kv, reach, start, norm_gains, out_weight):
    nodes, width = query.shape
    rows = 128
    span = rows + 2 * BAND
    vmem = pl.BlockSpec(memory_space=pltpu.VMEM)
    return pl.pallas_call(
        attention_kernel,
        out_shape=(
            jax.ShapeDtypeStruct((nodes, width), F32),
            jax.ShapeDtypeStruct((nodes, width), BF16),
        ),
        in_specs=[pl.BlockSpec(memory_space=pltpu.SMEM)]
        + [vmem] * 5
        + [pl.BlockSpec(memory_space=pl.ANY)],
        scratch_shapes=[
            pltpu.VMEM((nodes // rows, rows, span), F32),
            pltpu.VMEM((nodes, width), BF16),
            pltpu.VMEM(out_weight.shape, BF16),
            pltpu.SemaphoreType.DMA,
        ],
        compiler_params=params(32),
        cost_estimate=cost(
            4 * nodes * span * width + 2 * nodes * width * width,
            10 << 20,
            nodes * span * HEADS,
        ),
        name="attention",
    )(where, query, kv, reach, start, norm_gains, out_weight)


def in_order_kernel(place_ref, *refs):
    out_ref = refs[-1]
    count = len(refs) - 1
    for shift in range(count):
        out_ref[lax.rem(place_ref[4] + shift, count)] = refs[shift][...]


def in_order(place, blocks):
    count = len(blocks)
    vmem = pl.BlockSpec(memory_space=pltpu.VMEM)
    return pl.pallas_call(
        in_order_kernel,
        out_shape=jax.ShapeDtypeStruct((count,) + blocks[0].shape, BF16),
        in_specs=[pl.BlockSpec(memory_space=pltpu.SMEM)] + [vmem] * count,
        compiler_params=params(16),
        cost_estimate=cost(0, 2 * count * blocks[0].size * 2),
        name="shards_in_order",
    )(place, *blocks)


def mlp_kernel(place_ref, own_ref, other_ref, *refs):
    blocks = refs[:8]
    far = refs[8:10]
    own_out, other_out, tokens_ref, total_ref = refs[10:]
    nodes, width = own_ref.shape
    part = width // 8
    hidden = blocks[0].shape[2]
    rows = blocks[0].shape[1] // 2
    step = 512

    def at(block):
        along_x = lax.rem(place_ref[3] + (0, 3, 1, 2)[block % 4], 4)
        along_y = place_ref[5] if block < 4 else 1 - place_ref[5]
        return pl.ds(pl.multiple_of((along_y * 4 + along_x) * part, part), part)

    for block in range(8):
        columns = slice(block * part, (block + 1) * part)
        tokens_ref[:nodes, columns] = other_ref[:, at(block)]
        tokens_ref[nodes:, columns] = own_ref[:, at(block)]

    def all_rows(first, chosen):
        pieces = []
        for block in range(8):
            if block % 4 < 3:
                sources = (blocks[block - block // 4],)
            else:
                sources = ((blocks[6], blocks[7]), far)[block // 4]
            for source in sources:
                piece = source[:, first : first + rows, chosen]
                pieces.append(piece.reshape(piece.shape[0] * rows, step))
        return jnp.concatenate(pieces, axis=0)

    for start in range(0, hidden, step):
        chosen = slice(start, start + step)
        upper = dot(tokens_ref[...], all_rows(0, chosen))
        active = jax.nn.gelu(upper).astype(BF16)
        lowered = dot_lanes(active, all_rows(rows, chosen))
        if start == 0:
            total_ref[...] = lowered
        else:
            total_ref[...] += lowered
    for block in range(8):
        columns = slice(block * part, (block + 1) * part)
        other_out[:, at(block)] = total_ref[:nodes, columns]
        own_out[:, at(block)] = total_ref[nodes:, columns]


def mlp_parts(place, own, other, blocks):
    nodes, width = own.shape
    hidden = blocks[0].shape[2]
    vmem = pl.BlockSpec(memory_space=pltpu.VMEM)
    return pl.pallas_call(
        mlp_kernel,
        out_shape=(jax.ShapeDtypeStruct((nodes, width), F32),) * 2,
        in_specs=[pl.BlockSpec(memory_space=pltpu.SMEM)] + [vmem] * (2 + len(blocks)),
        scratch_shapes=[
            pltpu.VMEM((2 * nodes, width), BF16),
            pltpu.VMEM((2 * nodes, width), F32),
        ],
        compiler_params=params(40),
        cost_estimate=cost(8 * nodes * width * hidden, 12 << 20, 2 * nodes * hidden),
        name="mlp_parts",
    )(place, own, other, *blocks)


def gathered_shards(place, share):
    def turn(block, axis, step):
        count = lax.axis_size(axis)
        return lax.ppermute(block, axis, [(i, (i + step) % count) for i in range(count)])

    def beside(block):
        return lax.ppermute(block, NODE[0], [(0, 1), (1, 0)])

    def across(block):
        return lax.ppermute(
            block, (MEMBER[0], NODE[0]), [(0, 3), (3, 0), (1, 2), (2, 1)]
        )

    ahead, behind = [share], [share]
    for step in range(4):
        ahead.append(turn(ahead[-1], NODE[2], 1))
        if step < 3:
            behind.append(turn(behind[-1], NODE[2], -1))
    column = in_order(
        place, [share] + behind[1:] + [ahead[4], ahead[3], ahead[2], ahead[1]]
    )
    before = turn(column, NODE[1], 1)
    after = turn(column, NODE[1], -1)
    half = column.shape[0] // 2
    far_low = turn(before[:half], NODE[1], 1)
    far_high = turn(after[half:], NODE[1], -1)
    return (
        column,
        before,
        after,
        beside(column),
        beside(before),
        across(after),
        far_low,
        far_high,
        beside(far_low),
        across(far_high),
    )


def head_kernel(mid_ref, own_ref, other_ref, gain_ref, head_ref, out_ref):
    ending = mid_ref[...] + (own_ref[...] + other_ref[...])
    final = layer_norm(ending, gain_ref[2:3, :]).astype(BF16)
    out_ref[...] = dot_lanes(head_ref[...], final).astype(BF16)


def head(middle, own, other, norm_gains, head_rows):
    nodes, width = middle.shape
    variables = head_rows.shape[0]
    return pl.pallas_call(
        head_kernel,
        out_shape=jax.ShapeDtypeStruct((variables, nodes), BF16),
        compiler_params=params(24),
        cost_estimate=cost(2 * nodes * width * variables, 4 << 20),
        name="final_head",
    )(middle, own, other, norm_gains, head_rows)


def decoder_tally_kernel(place_ref, slots_ref, out_ref):
    rows = 64
    points = out_ref.shape[1]
    slots = slots_ref.shape[0]

    def body(step, carry):
        first = pl.multiple_of(step * rows, rows)
        node = first + place_ref[7] + lax.broadcasted_iota(jnp.int32, (rows, points), 0)
        total = jnp.zeros((rows, points), F32)
        for position in range(slots):
            hit = slots_ref[position : position + 1, :] == node
            total = total + jnp.where(hit, 1.0 / slots, 0.0)
        out_ref[pl.ds(first, rows), :] = total.astype(BF16)
        return carry

    lax.fori_loop(0, out_ref.shape[0] // rows, body, 0)


def decoder_tallies(place, slots, nodes):
    count, points = slots.shape
    return pl.pallas_call(
        decoder_tally_kernel,
        in_specs=[
            pl.BlockSpec(memory_space=pltpu.SMEM),
            pl.BlockSpec(memory_space=pltpu.VMEM),
        ],
        out_shape=jax.ShapeDtypeStruct((nodes, points), BF16),
        compiler_params=params(16),
        cost_estimate=cost(3 * nodes * points * count, nodes * points * 2),
        name="decoder_tallies",
    )(place, slots)


def crps_kernel(place_ref, tally_ref, state_ref, truth_ref, low_ref, own_ref, high_ref, out_ref, field_ref):
    members, variables, nodes = own_ref.shape
    state = state_ref[:variables, :].astype(F32)
    for member in range(members):
        field = dot(own_ref[member], tally_ref[nodes : 2 * nodes, :])
        field = field + dot(low_ref[member], tally_ref[:nodes, :])
        field = field + dot(high_ref[member], tally_ref[2 * nodes :, :])
        field_ref[member] = state + field
    own = field_ref[place_ref[6]]
    pairwise = None
    for member in range(members):
        term = score_gradient(own - field_ref[member])
        pairwise = term if pairwise is None else pairwise + term
    out_ref[0] = score_gradient(own - truth_ref[...].astype(F32)) * (
        1.0 / members
    ) - pairwise * (1.0 / (members * (members - 1)))


def crps(place, tallies, state, truth, low, own, high):
    variables, points = truth.shape
    vmem = pl.BlockSpec(memory_space=pltpu.VMEM)
    return pl.pallas_call(
        crps_kernel,
        out_shape=jax.ShapeDtypeStruct((1, variables, points), F32),
        in_specs=[pl.BlockSpec(memory_space=pltpu.SMEM)] + [vmem] * 6,
        scratch_shapes=[pltpu.VMEM((own.shape[0], variables, points), F32)],
        compiler_params=params(32),
        cost_estimate=cost(2 * 4 * variables * points * tallies.shape[0], 4 << 20),
        name="decoder_crps",
    )(place, tallies, state, truth, low, own, high)


def per_device(
    gridpoint_state,
    grid_truth,
    encoder_slots,
    encoder_count,
    node_reach,
    decoder_slots,
    member_perturb,
    embed_weight,
    norm_gains,
    qkv_weight,
    out_weight,
    up_weight,
    down_weight,
    head_weight,
):
    region = lax.axis_index(NODE)
    region_count = lax.axis_size(NODE)
    core = lax.axis_index("member_core")
    grid_dev = gridpoint_state.shape[1]
    node_dev = encoder_slots.shape[0]
    hidden = up_weight.shape[1] // 2
    perturb = member_perturb[0]

    place = jnp.stack(
        [
            region * node_dev,
            region_count * node_dev,
            (region - 1) * grid_dev,
            lax.axis_index(NODE[1]),
            lax.axis_index(NODE[2]),
            lax.axis_index(NODE[0]),
            lax.axis_index(MEMBER),
            (region - 1) * node_dev,
        ]
    ).astype(jnp.int32)

    state_low, state_high = neighbours(gridpoint_state)

    share = jnp.concatenate(
        [
            lax.dynamic_slice_in_dim(up_weight, core * hidden, hidden, 1),
            lax.dynamic_slice_in_dim(down_weight, core * hidden, hidden, 1),
        ],
        axis=0,
    )
    shards = gathered_shards(place, share)
    perturb_low, perturb_high = neighbours(perturb)

    counts = encoder_count[None, :]
    tallies = encoder_tallies(place, encoder_slots.T, counts, 3 * grid_dev)
    decoder_near = decoder_tallies(place, decoder_slots.T, 3 * node_dev)
    pooled = pool(tallies, state_low, gridpoint_state, state_high, counts)
    pooled_low, pooled_high = neighbours(pooled)
    start, query, kv = qkv(
        (pooled_low, pooled, pooled_high),
        (perturb_low, perturb, perturb_high),
        embed_weight,
        norm_gains,
        qkv_weight,
    )
    middle, normed_mid = attention(
        place, query, kv, node_reach[None, :], start, norm_gains, out_weight
    )

    normed_other = other_core(normed_mid)
    part_mine, part_other = mlp_parts(place, normed_mid, normed_other, shards)
    projected = head(middle, part_mine, other_core(part_other), norm_gains, head_weight.T)

    projected_all = lax.all_gather(projected, MEMBER, axis=0)
    projected_low, projected_high = neighbours(projected_all)
    return crps(
        place,
        decoder_near,
        gridpoint_state,
        grid_truth,
        projected_low,
        projected_all,
        projected_high,
    )


def solution(mesh):
    torus = Mesh(
        mesh.devices.reshape(2, 2, 2, 4, 8),
        MEMBER + NODE,
    )
    return jax.shard_map(
        per_device,
        mesh=torus,
        in_specs=(
            P(None, NODE),
            P(None, NODE),
            P(NODE, None),
            P(NODE),
            P(NODE),
            P(NODE, None),
            P(MEMBER, NODE, None),
            P(),
            P(),
            P(),
            P(),
            P(NODE, None),
            P(NODE, None),
            P(),
        ),
        out_specs=P(MEMBER, None, NODE),
        check_vma=False,
    )
```

```python
import jax
import jax.numpy as jnp
from jax import lax
from jax.experimental import pallas as pl
from jax.experimental.pallas import tpu as pltpu
from jax.sharding import Mesh
from jax.sharding import PartitionSpec as P

HEADS = 16
HEAD_DIM = 64
BAND = 256
NODE = ("node_0", "node_1", "node_2")
MEMBER = ("member_hi", "member_core")

EPS = 1e-05
SMOOTH = 0.25

F32 = jnp.float32
BF16 = jnp.bfloat16
LANES_BOTH = (((1,), (1,)), ((), ()))


def params(mib):
    return pltpu.CompilerParams(vmem_limit_bytes=mib * 1024 * 1024)


SHORT = pl.CostEstimate(flops=1, bytes_accessed=1, transcendentals=0)


def layer_norm(entries, scale_gain):
    average = jnp.mean(entries, axis=-1, keepdims=True)
    centred = entries - average
    variance = jnp.mean(centred * centred, axis=-1, keepdims=True)
    return centred * lax.rsqrt(variance + EPS) * scale_gain


def score_gradient(difference):
    return difference * lax.rsqrt(difference * difference + SMOOTH * SMOOTH)


def dot(left_side, right_side):
    return jnp.dot(left_side, right_side, preferred_element_type=F32)


def dot_lanes(left_side, right_side):
    return lax.dot_general(left_side, right_side, LANES_BOTH, preferred_element_type=F32)


def neighbours(block):
    count = lax.axis_size(NODE)
    forward = [(i, (i + 1) % count) for i in range(count)]
    backward = [(target, source) for source, target in forward]
    return lax.ppermute(block, NODE, forward), lax.ppermute(block, NODE, backward)


def other_core(block):
    return lax.ppermute(block, "member_core", [(0, 1), (1, 0)])


def tally_kernel(place_ref, slots_ref, count_ref, out_ref):
    rows = 64
    nodes = out_ref.shape[1]
    slots = slots_ref[...] - place_ref[2]
    used = lax.broadcasted_iota(jnp.int32, slots.shape, 0) < count_ref[...]
    slots = jnp.where(used, slots, -1)

    def body(step, carry):
        first = pl.multiple_of(step * rows, rows)
        window = first + lax.broadcasted_iota(jnp.int32, (rows, nodes), 0)
        total = jnp.zeros((rows, nodes), F32)
        for position in range(slots.shape[0]):
            hit = slots[position : position + 1, :] == window
            total = total + jnp.where(hit, 1.0, 0.0)
        out_ref[pl.ds(first, rows), :] = total.astype(BF16)
        return carry

    lax.fori_loop(0, out_ref.shape[0] // rows, body, 0)


def encoder_tallies(place, slots, counts, width):
    count, nodes = slots.shape
    vmem = pl.BlockSpec(memory_space=pltpu.VMEM)
    return pl.pallas_call(
        tally_kernel,
        out_shape=jax.ShapeDtypeStruct((width, nodes), BF16),
        in_specs=[pl.BlockSpec(memory_space=pltpu.SMEM), vmem, vmem],
        compiler_params=params(16),
        cost_estimate=SHORT,
        name="encoder_tallies",
    )(place, slots, counts)


def pooled_kernel(tally_ref, low_ref, own_ref, high_ref, count_ref, out_ref):
    width = low_ref.shape[1]
    total = dot(own_ref[...], tally_ref[width : 2 * width, :])
    total = total + dot(low_ref[...], tally_ref[:width, :])
    total = total + dot(high_ref[...], tally_ref[2 * width :, :])
    out_ref[...] = (total / count_ref[...].astype(F32)).astype(BF16)


def pool(tallies, low, own, high, counts):
    nodes = tallies.shape[1]
    channels = own.shape[0]
    return pl.pallas_call(
        pooled_kernel,
        out_shape=jax.ShapeDtypeStruct((channels, nodes), BF16),
        compiler_params=params(24),
        cost_estimate=SHORT,
        name="pooled",
    )(tallies, low, own, high, counts)


def qkv_kernel(
    pool_low, pool_own, pool_high, per_low, per_own, per_high, embed_ref, gain_ref, qkv_hbm,
    start_ref, query_ref, kv_ref, qkv_ref, sem,
):
    copy = pltpu.make_async_copy(qkv_hbm, qkv_ref, sem)
    copy.start()
    nodes, width = start_ref.shape
    gain = gain_ref[0:1, :]

    def start_of(pooled, perturb):
        embedded = lax.dot_general(
            pooled[...], embed_ref[...], (((0,), (0,)), ((), ())), preferred_element_type=F32
        )
        return embedded + perturb[...].astype(F32)

    normed = []
    for place, (pooled, perturb) in enumerate(
        ((pool_low, per_low), (pool_own, per_own), (pool_high, per_high))
    ):
        start = start_of(pooled, perturb)
        if place == 1:
            start_ref[...] = start
        normed.append(layer_norm(start, gain).astype(BF16))
    copy.wait()
    query = dot(normed[1], qkv_ref[:, :width]).astype(BF16)
    query_ref[...] = query * jnp.asarray(HEAD_DIM ** (-0.5), BF16)
    for place in range(3):
        for half in range(2):
            columns = slice((half + 1) * width, (half + 2) * width)
            kv_ref[place * nodes : (place + 1) * nodes, half * width : (half + 1) * width] = dot(
                normed[place], qkv_ref[:, columns]
            ).astype(BF16)


def qkv(pooled, perturbs, embed_weight, norm_gains, qkv_weight):
    nodes, width = perturbs[1].shape
    vmem = pl.BlockSpec(memory_space=pltpu.VMEM)
    return pl.pallas_call(
        qkv_kernel,
        out_shape=(
            jax.ShapeDtypeStruct((nodes, width), F32),
            jax.ShapeDtypeStruct((nodes, width), BF16),
            jax.ShapeDtypeStruct((3 * nodes, 2 * width), BF16),
        ),
        in_specs=[vmem] * 8 + [pl.BlockSpec(memory_space=pl.ANY)],
        scratch_shapes=[pltpu.VMEM(qkv_weight.shape, BF16), pltpu.SemaphoreType.DMA],
        compiler_params=params(44),
        cost_estimate=SHORT,
        name="embed_qkv",
    )(*pooled, *perturbs, embed_weight, norm_gains, qkv_weight)


def masked_caps(where_ref, reach_ref, cap_ref):
    blocks, rows, span = cap_ref.shape
    first_query = where_ref[0]
    node_total = where_ref[1]
    reaches = jnp.transpose(jnp.broadcast_to(reach_ref[...].astype(F32), (128, blocks * rows)))
    for block in range(blocks):
        at = first_query + block * rows + lax.broadcasted_iota(jnp.int32, (rows, span), 0)
        key = first_query - BAND + block * rows + lax.broadcasted_iota(jnp.int32, (rows, span), 1)
        reach = reaches[block * rows : (block + 1) * rows, :1].astype(jnp.int32)
        allowed = (jnp.abs(at - key) <= reach) & (key >= 0) & (key < node_total)
        cap_ref[block] = jnp.where(allowed, 3e38, -1e30)


def attend(query_ref, kv_ref, cap_ref, attended_ref, first_pair, pairs):
    blocks, rows, span = cap_ref.shape
    width = query_ref.shape[1]
    lane = lax.broadcasted_iota(jnp.int32, (1, 2 * HEAD_DIM), 1)
    for block in range(blocks):
        cap = cap_ref.at[block]
        for pair in range(first_pair, first_pair + pairs):
            columns = slice(pair * 2 * HEAD_DIM, (pair + 1) * 2 * HEAD_DIM)
            value_columns = slice(width + pair * 2 * HEAD_DIM, width + (pair + 1) * 2 * HEAD_DIM)
            queries = query_ref[block * rows : (block + 1) * rows, columns]
            keys = kv_ref[block * rows : block * rows + span, columns]
            values = kv_ref[block * rows : block * rows + span, value_columns]
            halves = []
            for side in range(2):
                mine = (lane < HEAD_DIM) if side == 0 else (lane >= HEAD_DIM)
                chosen = jnp.where(mine, queries, jnp.zeros_like(queries))
                scores = jnp.minimum(dot_lanes(chosen, keys), cap[...])
                highest = jnp.max(scores, axis=-1, keepdims=True)
                weights = jnp.exp(scores - highest)
                total = jnp.sum(weights, axis=-1, keepdims=True)
                blended = dot(weights.astype(BF16), values)
                halves.append(blended * (1.0 / total))
            attended_ref[block * rows : (block + 1) * rows, columns] = jnp.where(
                lane < HEAD_DIM, halves[0], halves[1]
            ).astype(BF16)


def first_heads_kernel(where_ref, query_ref, kv_ref, reach_ref, attended_ref, cap_ref):
    masked_caps(where_ref, reach_ref, cap_ref)
    attend(query_ref, kv_ref, cap_ref, attended_ref, 0, HEADS // 4)


def last_heads_kernel(
    where_ref, query_ref, kv_ref, cap_ref, first_ref, start_ref, gain_ref, out_hbm,
    mid_ref, normed_ref, attended_ref, out_ref, sem,
):
    copy = pltpu.make_async_copy(out_hbm, out_ref, sem)
    copy.start()
    attend(query_ref, kv_ref, cap_ref, attended_ref, HEADS // 4, HEADS // 4)
    copy.wait()
    half = first_ref.shape[1]
    middle = start_ref[...] + dot(first_ref[...], out_ref[:half, :])
    middle = middle + dot(attended_ref[:, half:], out_ref[half:, :])
    mid_ref[...] = middle
    normed_ref[...] = layer_norm(middle, gain_ref[1:2, :]).astype(BF16)


def first_heads(where, query, kv, reach):
    nodes, width = query.shape
    rows = 128
    span = rows + 2 * BAND
    vmem = pl.BlockSpec(memory_space=pltpu.VMEM)
    return pl.pallas_call(
        first_heads_kernel,
        out_shape=(
            jax.ShapeDtypeStruct((nodes, width // 2), BF16),
            jax.ShapeDtypeStruct((nodes // rows, rows, span), F32),
        ),
        in_specs=[pl.BlockSpec(memory_space=pltpu.SMEM)] + [vmem] * 3,
        compiler_params=params(24),
        cost_estimate=SHORT,
        name="first_heads",
    )(where, query, kv, reach)


def last_heads(where, query, kv, caps, first, start, norm_gains, out_weight):
    nodes, width = query.shape
    vmem = pl.BlockSpec(memory_space=pltpu.VMEM)
    return pl.pallas_call(
        last_heads_kernel,
        out_shape=(
            jax.ShapeDtypeStruct((nodes, width), F32),
            jax.ShapeDtypeStruct((nodes, width), BF16),
        ),
        in_specs=[pl.BlockSpec(memory_space=pltpu.SMEM)]
        + [vmem] * 6
        + [pl.BlockSpec(memory_space=pl.ANY)],
        scratch_shapes=[
            pltpu.VMEM((nodes, width), BF16),
            pltpu.VMEM(out_weight.shape, BF16),
            pltpu.SemaphoreType.DMA,
        ],
        compiler_params=params(24),
        cost_estimate=SHORT,
        name="last_heads",
    )(where, query, kv, caps, first, start, norm_gains, out_weight)


def in_order_kernel(place_ref, *refs):
    count = len(refs) - 2
    for shift in range(count):
        at = lax.rem(place_ref[4] + shift, count)
        for side in range(2):
            refs[count + side][at] = refs[shift][side]


def in_order(place, blocks):
    count = len(blocks)
    vmem = pl.BlockSpec(memory_space=pltpu.VMEM)
    return pl.pallas_call(
        in_order_kernel,
        out_shape=(jax.ShapeDtypeStruct((count,) + blocks[0].shape[1:], BF16),) * 2,
        in_specs=[pl.BlockSpec(memory_space=pltpu.SMEM)] + [vmem] * count,
        compiler_params=params(24),
        cost_estimate=SHORT,
        name="shards_in_order",
    )(place, *blocks)


def mlp_kernel(place_ref, own_ref, other_ref, *refs):
    blocks = refs[:8]
    own_out, other_out, tokens_ref, total_ref = refs[8:]
    nodes, width = own_ref.shape
    part = width // 8
    hidden = blocks[0].shape[2]
    rows = blocks[0].shape[1] // 2
    step = 512

    def at(block):
        along_x = lax.rem(place_ref[3] + (0, 3, 1, 2)[block % 4], 4)
        along_y = place_ref[5] if block < 4 else 1 - place_ref[5]
        return pl.ds(pl.multiple_of((along_y * 4 + along_x) * part, part), part)

    for block in range(8):
        columns = slice(block * part, (block + 1) * part)
        tokens_ref[:nodes, columns] = other_ref[:, at(block)]
        tokens_ref[nodes:, columns] = own_ref[:, at(block)]

    def all_rows(first, chosen):
        pieces = []
        for block in blocks:
            piece = block[:, first : first + rows, chosen]
            pieces.append(piece.reshape(piece.shape[0] * rows, step))
        return jnp.concatenate(pieces, axis=0)

    for start in range(0, hidden, step):
        chosen = slice(start, start + step)
        upper = dot(tokens_ref[...], all_rows(0, chosen))
        active = jax.nn.gelu(upper).astype(BF16)
        lowered = dot_lanes(active, all_rows(rows, chosen))
        if start == 0:
            total_ref[...] = lowered
        else:
            total_ref[...] += lowered
    for block in range(8):
        columns = slice(block * part, (block + 1) * part)
        other_out[:, at(block)] = total_ref[:nodes, columns]
        own_out[:, at(block)] = total_ref[nodes:, columns]


def mlp_parts(place, own, other, blocks):
    nodes, width = own.shape
    hidden = blocks[0].shape[2]
    vmem = pl.BlockSpec(memory_space=pltpu.VMEM)
    return pl.pallas_call(
        mlp_kernel,
        out_shape=(jax.ShapeDtypeStruct((nodes, width), F32),) * 2,
        in_specs=[pl.BlockSpec(memory_space=pltpu.SMEM)] + [vmem] * (2 + len(blocks)),
        scratch_shapes=[
            pltpu.VMEM((2 * nodes, width), BF16),
            pltpu.VMEM((2 * nodes, width), F32),
        ],
        compiler_params=params(40),
        cost_estimate=SHORT,
        name="mlp_parts",
    )(place, own, other, *blocks)


def turn(block, axis, step):
    count = lax.axis_size(axis)
    return lax.ppermute(block, axis, [(i, (i + step) % count) for i in range(count)])


def beside(block):
    return lax.ppermute(block, NODE[0], [(0, 1), (1, 0)])


def across(block):
    return lax.ppermute(block, (MEMBER[0], NODE[0]), [(0, 3), (3, 0), (1, 2), (2, 1)])


def head_kernel(mid_ref, own_ref, other_ref, gain_ref, head_ref, out_ref):
    ending = mid_ref[...] + (own_ref[...] + other_ref[...])
    final = layer_norm(ending, gain_ref[2:3, :]).astype(BF16)
    out_ref[...] = dot_lanes(head_ref[...], final).astype(BF16)


def head(middle, own, other, norm_gains, head_rows):
    nodes, width = middle.shape
    variables = head_rows.shape[0]
    return pl.pallas_call(
        head_kernel,
        out_shape=jax.ShapeDtypeStruct((variables, nodes), BF16),
        compiler_params=params(24),
        cost_estimate=SHORT,
        name="final_head",
    )(middle, own, other, norm_gains, head_rows)


def decoder_tally_kernel(place_ref, slots_ref, out_ref):
    rows = 64
    points = out_ref.shape[1]
    slots = slots_ref.shape[0]

    def body(step, carry):
        first = pl.multiple_of(step * rows, rows)
        node = first + place_ref[7] + lax.broadcasted_iota(jnp.int32, (rows, points), 0)
        total = jnp.zeros((rows, points), F32)
        for position in range(slots):
            hit = slots_ref[position : position + 1, :] == node
            total = total + jnp.where(hit, 1.0 / slots, 0.0)
        out_ref[pl.ds(first, rows), :] = total.astype(BF16)
        return carry

    lax.fori_loop(0, out_ref.shape[0] // rows, body, 0)


def decoder_tallies(place, slots, nodes):
    count, points = slots.shape
    return pl.pallas_call(
        decoder_tally_kernel,
        in_specs=[
            pl.BlockSpec(memory_space=pltpu.SMEM),
            pl.BlockSpec(memory_space=pltpu.VMEM),
        ],
        out_shape=jax.ShapeDtypeStruct((nodes, points), BF16),
        compiler_params=params(16),
        cost_estimate=SHORT,
        name="decoder_tallies",
    )(place, slots)


def crps_kernel(tally_ref, state_ref, truth_ref, *refs):
    out_ref, forecast_ref = refs[-2:]
    field_refs = refs[:-2]
    per_ref, padded, nodes = field_refs[0].shape
    variables = truth_ref.shape[0]
    state = state_ref[:variables, :].astype(F32)
    members = 0
    for first in range(0, len(field_refs), 3):
        delta = None
        for at in range(3):
            stacked = field_refs[first + at][...].reshape(per_ref * padded, nodes)
            term = dot(stacked, tally_ref[at * nodes : (at + 1) * nodes, :])
            delta = term if delta is None else delta + term
        for k in range(per_ref):
            forecast_ref[members] = state + delta[k * padded : k * padded + variables]
            members += 1
    own = forecast_ref[0]
    pairwise = None
    for member in range(members):
        term = score_gradient(own - forecast_ref[member])
        pairwise = term if pairwise is None else pairwise + term
    gradient = score_gradient(own - truth_ref[...].astype(F32)) * (1.0 / members) - pairwise * (
        1.0 / (members * (members - 1))
    )
    out_ref[...] = gradient[:, None, :]


def crps(tallies, state, truth, fields):
    variables, points = truth.shape
    members = len(fields) // 3 * fields[0].shape[0]
    return pl.pallas_call(
        crps_kernel,
        out_shape=jax.ShapeDtypeStruct((variables, 1, points), F32),
        scratch_shapes=[pltpu.VMEM((members, variables, points), F32)],
        compiler_params=params(32),
        cost_estimate=SHORT,
        name="decoder_crps",
    )(tallies, state, truth, *fields)


def per_device(
    gridpoint_state,
    grid_truth,
    encoder_slots,
    encoder_count,
    node_reach,
    decoder_slots,
    member_perturb,
    embed_weight,
    norm_gains,
    qkv_weight,
    out_weight,
    up_weight,
    down_weight,
    head_weight,
):
    region = lax.axis_index(NODE)
    region_count = lax.axis_size(NODE)
    core = lax.axis_index("member_core")
    grid_dev = gridpoint_state.shape[1]
    node_dev = encoder_slots.shape[0]
    hidden = up_weight.shape[1] // 2
    perturb = member_perturb[0]

    place = jnp.stack(
        [
            region * node_dev,
            region_count * node_dev,
            (region - 1) * grid_dev,
            lax.axis_index(NODE[1]),
            lax.axis_index(NODE[2]),
            lax.axis_index(NODE[0]),
            lax.axis_index(MEMBER),
            (region - 1) * node_dev,
        ]
    ).astype(jnp.int32)

    share = jnp.concatenate(
        [
            lax.dynamic_slice_in_dim(up_weight, core * hidden, hidden, 1),
            lax.dynamic_slice_in_dim(down_weight, core * hidden, hidden, 1),
        ],
        axis=0,
    )
    counts = encoder_count[None, :]
    tie = lax.optimization_barrier

    far_share = turn(share, NODE[1], 2)
    state_low, state_high = neighbours(gridpoint_state)
    both = jnp.stack([share, far_share])
    ahead, behind = [turn(both, NODE[2], 1)], [turn(both, NODE[2], -1)]
    tallies = encoder_tallies(place, encoder_slots.T, counts, 3 * grid_dev)
    tallies, ahead[0], behind[0] = tie((tallies, ahead[0], behind[0]))
    ahead.append(turn(ahead[-1], NODE[2], 1))
    behind.append(turn(behind[-1], NODE[2], -1))
    pooled = pool(tallies, state_low, gridpoint_state, state_high, counts)
    pooled, ahead[1], behind[1] = tie((pooled, ahead[1], behind[1]))
    pooled_low, pooled_high = neighbours(pooled)
    ahead.append(turn(ahead[-1], NODE[2], 1))
    behind.append(turn(behind[-1], NODE[2], -1))
    ahead.append(turn(ahead[-1], NODE[2], 1))
    column, far = in_order(place, [both] + behind + ahead[::-1])

    column, far, perturb, pooled_low, pooled_high = tie(
        (column, far, perturb, pooled_low, pooled_high)
    )
    before = turn(column, NODE[1], 1)
    after = turn(column, NODE[1], -1)
    other_column = beside(column)
    other_far = across(far)
    perturb_low, perturb_high = neighbours(perturb)
    start, query, kv = qkv(
        (pooled_low, pooled, pooled_high),
        (perturb_low, perturb, perturb_high),
        embed_weight,
        norm_gains,
        qkv_weight,
    )
    heads, caps = first_heads(place, query, kv, node_reach[None, :])
    decoder_near = decoder_tallies(place, decoder_slots.T, 3 * node_dev)
    heads, before, after, other_column, other_far, decoder_near = tie(
        (heads, before, after, other_column, other_far, decoder_near)
    )

    other_before = beside(before)
    other_after = across(after)
    middle, normed_mid = last_heads(
        place, query, kv, caps, heads, start, norm_gains, out_weight
    )
    shards = (
        column,
        before,
        after,
        far,
        other_column,
        other_before,
        other_after,
        other_far,
    )

    normed_other = other_core(normed_mid)
    part_mine, part_other = mlp_parts(place, normed_mid, normed_other, shards)
    head_rows = jnp.pad(head_weight.T, ((0, -head_weight.shape[1] % 16), (0, 0)))
    projected = head(middle, part_mine, other_core(part_other), norm_gains, head_rows)

    fields = jnp.stack([projected, other_core(projected)])

    def sent(step, flip):
        links = [
            (
                side * region_count + i,
                (side ^ flip) * region_count + (i + step) % region_count,
            )
            for side in range(2)
            for i in range(region_count)
        ]
        return lax.ppermute(fields, (MEMBER[0],) + NODE, links)

    near = (sent(1, 0), fields, sent(-1, 0))
    across_members = (sent(1, 1), sent(0, 1), sent(-1, 1))
    gradient = crps(
        decoder_near, gridpoint_state, grid_truth, near + across_members
    )
    return gradient.transpose(1, 0, 2)


def solution(mesh):
    torus = Mesh(
        mesh.devices.reshape(2, 2, 2, 4, 8),
        MEMBER + NODE,
    )
    return jax.shard_map(
        per_device,
        mesh=torus,
        in_specs=(
            P(None, NODE),
            P(None, NODE),
            P(NODE, None),
            P(NODE),
            P(NODE),
            P(NODE, None),
            P(MEMBER, NODE, None),
            P(),
            P(),
            P(),
            P(),
            P(NODE, None),
            P(NODE, None),
            P(),
        ),
        out_specs=P(MEMBER, None, NODE),
        check_vma=False,
    )
```

```python
import jax
import jax.numpy as jnp
from jax import lax
from jax.experimental import pallas as pl
from jax.experimental.pallas import tpu as pltpu
from jax.sharding import Mesh
from jax.sharding import PartitionSpec as P

HEADS = 16
HEAD_DIM = 64
BAND = 256
NODE = ("node_0", "node_1", "node_2")
MEMBER = ("member_hi", "member_core")

EPS = 1e-05
SMOOTH = 0.25

F32 = jnp.float32
BF16 = jnp.bfloat16
LANES_BOTH = (((1,), (1,)), ((), ()))


def params(mib):
    return pltpu.CompilerParams(vmem_limit_bytes=mib * 1024 * 1024)


SHORT = pl.CostEstimate(flops=1, bytes_accessed=1, transcendentals=0)


def layer_norm(entries, scale_gain):
    average = jnp.mean(entries, axis=-1, keepdims=True)
    centred = entries - average
    variance = jnp.mean(centred * centred, axis=-1, keepdims=True)
    return centred * lax.rsqrt(variance + EPS) * scale_gain


def score_gradient(difference):
    return difference * lax.rsqrt(difference * difference + SMOOTH * SMOOTH)


def dot(left_side, right_side):
    return jnp.dot(left_side, right_side, preferred_element_type=F32)


def dot_lanes(left_side, right_side):
    return lax.dot_general(left_side, right_side, LANES_BOTH, preferred_element_type=F32)


def neighbours(block):
    count = lax.axis_size(NODE)
    forward = [(i, (i + 1) % count) for i in range(count)]
    backward = [(target, source) for source, target in forward]
    return lax.ppermute(block, NODE, forward), lax.ppermute(block, NODE, backward)


def other_core(block):
    return lax.ppermute(block, "member_core", [(0, 1), (1, 0)])


def tally_kernel(place_ref, slots_ref, count_ref, out_ref):
    nodes = out_ref.shape[1]
    tall, rows = 256, 64
    slots = slots_ref[...] - place_ref[2]
    used = lax.broadcasted_iota(jnp.int32, slots.shape, 0) < count_ref[...]
    slots = jnp.where(used, slots, -1)
    high = slots >> 8
    low = (slots & 255).astype(F32)
    window = lax.broadcasted_iota(jnp.int32, (tall, nodes), 0).astype(F32).astype(BF16)
    one, zero = jnp.ones((), BF16), jnp.zeros((), BF16)

    def body(step, carry):
        first = pl.multiple_of(step * tall, tall)
        keys = jnp.where(high == step, low, -1.0).astype(BF16)
        for start in range(0, tall, rows):
            total = jnp.zeros((rows, nodes), BF16)
            for position in range(slots.shape[0]):
                hit = keys[position : position + 1, :] == window[start : start + rows, :]
                total = total + jnp.where(hit, one, zero)
            out_ref[pl.ds(first + start, rows), :] = total
        return carry

    lax.fori_loop(0, out_ref.shape[0] // tall, body, 0)


def encoder_tallies(place, slots, counts, width):
    count, nodes = slots.shape
    vmem = pl.BlockSpec(memory_space=pltpu.VMEM)
    return pl.pallas_call(
        tally_kernel,
        out_shape=jax.ShapeDtypeStruct((width, nodes), BF16),
        in_specs=[pl.BlockSpec(memory_space=pltpu.SMEM), vmem, vmem],
        compiler_params=params(16),
        cost_estimate=SHORT,
        name="encoder_tallies",
    )(place, slots, counts)


def pooled_kernel(tally_ref, low_ref, own_ref, high_ref, count_ref, out_ref):
    width = low_ref.shape[1]
    total = dot(own_ref[...], tally_ref[width : 2 * width, :])
    total = total + dot(low_ref[...], tally_ref[:width, :])
    total = total + dot(high_ref[...], tally_ref[2 * width :, :])
    out_ref[...] = (total / count_ref[...].astype(F32)).astype(BF16)


def pool(tallies, low, own, high, counts):
    nodes = tallies.shape[1]
    channels = own.shape[0]
    return pl.pallas_call(
        pooled_kernel,
        out_shape=jax.ShapeDtypeStruct((channels, nodes), BF16),
        compiler_params=params(24),
        cost_estimate=SHORT,
        name="pooled",
    )(tallies, low, own, high, counts)


def embed_kernel(pooled_ref, perturb_ref, embed_ref, gain_ref, start_ref, normed_ref):
    embedded = lax.dot_general(
        pooled_ref[...], embed_ref[...], (((0,), (0,)), ((), ())), preferred_element_type=F32
    )
    start = embedded + perturb_ref[...].astype(F32)
    start_ref[...] = start
    normed_ref[...] = layer_norm(start, gain_ref[0:1, :]).astype(BF16)


def embed(pooled, perturb, embed_weight, norm_gains):
    return pl.pallas_call(
        embed_kernel,
        out_shape=(
            jax.ShapeDtypeStruct(perturb.shape, F32),
            jax.ShapeDtypeStruct(perturb.shape, BF16),
        ),
        compiler_params=params(16),
        cost_estimate=SHORT,
        name="embed",
    )(pooled, perturb, embed_weight, norm_gains)


def qkv_kernel(low_ref, own_ref, high_ref, qkv_hbm, query_ref, kv_ref, qkv_ref, sem):
    copy = pltpu.make_async_copy(qkv_hbm, qkv_ref, sem)
    copy.start()
    nodes, width = own_ref.shape
    copy.wait()
    query = dot(own_ref[...], qkv_ref[:, :width]).astype(BF16)
    query_ref[...] = query * jnp.asarray(HEAD_DIM ** (-0.5), BF16)
    for place, normed in enumerate((low_ref, own_ref, high_ref)):
        for half in range(2):
            columns = slice((half + 1) * width, (half + 2) * width)
            kv_ref[place * nodes : (place + 1) * nodes, half * width : (half + 1) * width] = dot(
                normed[...], qkv_ref[:, columns]
            ).astype(BF16)


def qkv(low, own, high, qkv_weight):
    nodes, width = own.shape
    vmem = pl.BlockSpec(memory_space=pltpu.VMEM)
    return pl.pallas_call(
        qkv_kernel,
        out_shape=(
            jax.ShapeDtypeStruct((nodes, width), BF16),
            jax.ShapeDtypeStruct((3 * nodes, 2 * width), BF16),
        ),
        in_specs=[vmem] * 3 + [pl.BlockSpec(memory_space=pl.ANY)],
        scratch_shapes=[pltpu.VMEM(qkv_weight.shape, BF16), pltpu.SemaphoreType.DMA],
        compiler_params=params(32),
        cost_estimate=SHORT,
        name="qkv",
    )(low, own, high, qkv_weight)


def attention_kernel(
    where_ref, query_ref, kv_ref, reach_ref, start_ref, gain_ref, out_hbm,
    mid_ref, normed_ref, cap_ref, attended_ref, out_ref, sem,
):
    copy = pltpu.make_async_copy(out_hbm, out_ref, sem)
    copy.start()
    nodes, width = query_ref.shape
    rows = cap_ref.shape[1]
    span = cap_ref.shape[2]
    first_query = where_ref[0]
    node_total = where_ref[1]
    reaches = jnp.transpose(jnp.broadcast_to(reach_ref[...].astype(F32), (128, nodes)))
    for block in range(nodes // rows):
        at = first_query + block * rows + lax.broadcasted_iota(jnp.int32, (rows, span), 0)
        key = first_query - BAND + block * rows + lax.broadcasted_iota(jnp.int32, (rows, span), 1)
        reach = reaches[block * rows : (block + 1) * rows, :1].astype(jnp.int32)
        allowed = (jnp.abs(at - key) <= reach) & (key >= 0) & (key < node_total)
        cap_ref[block] = jnp.where(allowed, 3e38, -1e30)

    lane = lax.broadcasted_iota(jnp.int32, (1, 2 * HEAD_DIM), 1)
    for block in range(nodes // rows):
        cap = cap_ref.at[block]
        for pair in range(HEADS // 2):
            columns = slice(pair * 2 * HEAD_DIM, (pair + 1) * 2 * HEAD_DIM)
            value_columns = slice(width + pair * 2 * HEAD_DIM, width + (pair + 1) * 2 * HEAD_DIM)
            queries = query_ref[block * rows : (block + 1) * rows, columns]
            keys = kv_ref[block * rows : block * rows + span, columns]
            values = kv_ref[block * rows : block * rows + span, value_columns]
            halves = []
            for side in range(2):
                mine = (lane < HEAD_DIM) if side == 0 else (lane >= HEAD_DIM)
                chosen = jnp.where(mine, queries, jnp.zeros_like(queries))
                scores = jnp.minimum(dot_lanes(chosen, keys), cap[...])
                highest = jnp.max(scores, axis=-1, keepdims=True)
                weights = jnp.exp(scores - highest)
                total = jnp.sum(weights, axis=-1, keepdims=True)
                blended = dot(weights.astype(BF16), values)
                halves.append(blended * (1.0 / total))
            attended_ref[block * rows : (block + 1) * rows, columns] = jnp.where(
                lane < HEAD_DIM, halves[0], halves[1]
            ).astype(BF16)
    copy.wait()
    middle = start_ref[...] + dot(attended_ref[...], out_ref[...])
    mid_ref[...] = middle
    normed_ref[...] = layer_norm(middle, gain_ref[1:2, :]).astype(BF16)


def attention(where, query, kv, reach, start, norm_gains, out_weight):
    nodes, width = query.shape
    rows = 128
    span = rows + 2 * BAND
    vmem = pl.BlockSpec(memory_space=pltpu.VMEM)
    return pl.pallas_call(
        attention_kernel,
        out_shape=(
            jax.ShapeDtypeStruct((nodes, width), F32),
            jax.ShapeDtypeStruct((nodes, width), BF16),
        ),
        in_specs=[pl.BlockSpec(memory_space=pltpu.SMEM)]
        + [vmem] * 5
        + [pl.BlockSpec(memory_space=pl.ANY)],
        scratch_shapes=[
            pltpu.VMEM((nodes // rows, rows, span), F32),
            pltpu.VMEM((nodes, width), BF16),
            pltpu.VMEM(out_weight.shape, BF16),
            pltpu.SemaphoreType.DMA,
        ],
        compiler_params=params(32),
        cost_estimate=SHORT,
        name="attention",
    )(where, query, kv, reach, start, norm_gains, out_weight)


def in_order_kernel(place_ref, *refs):
    count = len(refs) - 2
    for shift in range(count):
        at = lax.rem(place_ref[4] + shift, count)
        for side in range(2):
            refs[count + side][at] = refs[shift][side]


def in_order(place, blocks):
    count = len(blocks)
    vmem = pl.BlockSpec(memory_space=pltpu.VMEM)
    return pl.pallas_call(
        in_order_kernel,
        out_shape=(jax.ShapeDtypeStruct((count,) + blocks[0].shape[1:], BF16),) * 2,
        in_specs=[pl.BlockSpec(memory_space=pltpu.SMEM)] + [vmem] * count,
        compiler_params=params(24),
        cost_estimate=SHORT,
        name="shards_in_order",
    )(place, *blocks)


def mlp_kernel(place_ref, own_ref, other_ref, *refs):
    blocks = refs[:8]
    own_out, other_out, tokens_ref, total_ref = refs[8:]
    nodes, width = own_ref.shape
    part = width // 8
    hidden = blocks[0].shape[2]
    rows = blocks[0].shape[1] // 2
    step = 512

    def at(block):
        along_x = lax.rem(place_ref[3] + (0, 3, 1, 2)[block % 4], 4)
        along_y = place_ref[5] if block < 4 else 1 - place_ref[5]
        return pl.ds(pl.multiple_of((along_y * 4 + along_x) * part, part), part)

    for block in range(8):
        columns = slice(block * part, (block + 1) * part)
        tokens_ref[:nodes, columns] = other_ref[:, at(block)]
        tokens_ref[nodes:, columns] = own_ref[:, at(block)]

    def all_rows(first, chosen):
        pieces = []
        for block in blocks:
            piece = block[:, first : first + rows, chosen]
            pieces.append(piece.reshape(piece.shape[0] * rows, step))
        return jnp.concatenate(pieces, axis=0)

    for start in range(0, hidden, step):
        chosen = slice(start, start + step)
        upper = dot(tokens_ref[...], all_rows(0, chosen))
        active = jax.nn.gelu(upper).astype(BF16)
        lowered = dot_lanes(active, all_rows(rows, chosen))
        if start == 0:
            total_ref[...] = lowered
        else:
            total_ref[...] += lowered
    for block in range(8):
        columns = slice(block * part, (block + 1) * part)
        other_out[:, at(block)] = total_ref[:nodes, columns]
        own_out[:, at(block)] = total_ref[nodes:, columns]


def mlp_parts(place, own, other, blocks):
    nodes, width = own.shape
    hidden = blocks[0].shape[2]
    vmem = pl.BlockSpec(memory_space=pltpu.VMEM)
    return pl.pallas_call(
        mlp_kernel,
        out_shape=(jax.ShapeDtypeStruct((nodes, width), F32),) * 2,
        in_specs=[pl.BlockSpec(memory_space=pltpu.SMEM)] + [vmem] * (2 + len(blocks)),
        scratch_shapes=[
            pltpu.VMEM((2 * nodes, width), BF16),
            pltpu.VMEM((2 * nodes, width), F32),
        ],
        compiler_params=params(40),
        cost_estimate=SHORT,
        name="mlp_parts",
    )(place, own, other, *blocks)


def turn(block, axis, step):
    count = lax.axis_size(axis)
    return lax.ppermute(block, axis, [(i, (i + step) % count) for i in range(count)])


def beside(block):
    return lax.ppermute(block, NODE[0], [(0, 1), (1, 0)])


def across(block):
    return lax.ppermute(block, (MEMBER[0], NODE[0]), [(0, 3), (3, 0), (1, 2), (2, 1)])


def head_kernel(mid_ref, own_ref, other_ref, gain_ref, head_ref, out_ref):
    ending = mid_ref[...] + (own_ref[...] + other_ref[...])
    final = layer_norm(ending, gain_ref[2:3, :]).astype(BF16)
    out_ref[...] = dot_lanes(head_ref[...], final).astype(BF16)


def head(middle, own, other, norm_gains, head_rows):
    nodes, width = middle.shape
    variables = head_rows.shape[0]
    return pl.pallas_call(
        head_kernel,
        out_shape=jax.ShapeDtypeStruct((variables, nodes), BF16),
        compiler_params=params(24),
        cost_estimate=SHORT,
        name="final_head",
    )(middle, own, other, norm_gains, head_rows)


def decoder_tally_kernel(place_ref, slots_ref, out_ref):
    rows = 64
    points = out_ref.shape[1]
    slots = slots_ref.shape[0]

    def body(step, carry):
        first = pl.multiple_of(step * rows, rows)
        node = first + place_ref[7] + lax.broadcasted_iota(jnp.int32, (rows, points), 0)
        total = jnp.zeros((rows, points), F32)
        for position in range(slots):
            hit = slots_ref[position : position + 1, :] == node
            total = total + jnp.where(hit, 1.0 / slots, 0.0)
        out_ref[pl.ds(first, rows), :] = total.astype(BF16)
        return carry

    lax.fori_loop(0, out_ref.shape[0] // rows, body, 0)


def decoder_tallies(place, slots, nodes):
    count, points = slots.shape
    return pl.pallas_call(
        decoder_tally_kernel,
        in_specs=[
            pl.BlockSpec(memory_space=pltpu.SMEM),
            pl.BlockSpec(memory_space=pltpu.VMEM),
        ],
        out_shape=jax.ShapeDtypeStruct((nodes, points), BF16),
        compiler_params=params(16),
        cost_estimate=SHORT,
        name="decoder_tallies",
    )(place, slots)


def crps_kernel(tally_ref, state_ref, truth_ref, *refs):
    out_ref, forecast_ref = refs[-2:]
    field_refs = refs[:-2]
    per_ref, padded, nodes = field_refs[0].shape
    variables = truth_ref.shape[0]
    state = state_ref[:variables, :].astype(F32)
    members = 0
    for first in range(0, len(field_refs), 3):
        delta = None
        for at in range(3):
            stacked = field_refs[first + at][...].reshape(per_ref * padded, nodes)
            term = dot(stacked, tally_ref[at * nodes : (at + 1) * nodes, :])
            delta = term if delta is None else delta + term
        for k in range(per_ref):
            forecast_ref[members] = state + delta[k * padded : k * padded + variables]
            members += 1
    own = forecast_ref[0]
    pairwise = None
    for member in range(members):
        term = score_gradient(own - forecast_ref[member])
        pairwise = term if pairwise is None else pairwise + term
    gradient = score_gradient(own - truth_ref[...].astype(F32)) * (1.0 / members) - pairwise * (
        1.0 / (members * (members - 1))
    )
    out_ref[...] = gradient[:, None, :]


def crps(tallies, state, truth, fields):
    variables, points = truth.shape
    members = len(fields) // 3 * fields[0].shape[0]
    return pl.pallas_call(
        crps_kernel,
        out_shape=jax.ShapeDtypeStruct((variables, 1, points), F32),
        scratch_shapes=[pltpu.VMEM((members, variables, points), F32)],
        compiler_params=params(32),
        cost_estimate=SHORT,
        name="decoder_crps",
    )(tallies, state, truth, *fields)


def per_device(
    gridpoint_state,
    grid_truth,
    encoder_slots,
    encoder_count,
    node_reach,
    decoder_slots,
    member_perturb,
    embed_weight,
    norm_gains,
    qkv_weight,
    out_weight,
    up_weight,
    down_weight,
    head_weight,
):
    region = lax.axis_index(NODE)
    region_count = lax.axis_size(NODE)
    core = lax.axis_index("member_core")
    grid_dev = gridpoint_state.shape[1]
    node_dev = encoder_slots.shape[0]
    hidden = up_weight.shape[1] // 2
    perturb = member_perturb[0]

    place = jnp.stack(
        [
            region * node_dev,
            region_count * node_dev,
            (region - 1) * grid_dev,
            lax.axis_index(NODE[1]),
            lax.axis_index(NODE[2]),
            lax.axis_index(NODE[0]),
            lax.axis_index(MEMBER),
            (region - 1) * node_dev,
        ]
    ).astype(jnp.int32)

    share = jnp.concatenate(
        [
            lax.dynamic_slice_in_dim(up_weight, core * hidden, hidden, 1),
            lax.dynamic_slice_in_dim(down_weight, core * hidden, hidden, 1),
        ],
        axis=0,
    )
    counts = encoder_count[None, :]
    tie = lax.optimization_barrier

    far_share = turn(share, NODE[1], 2)
    state_low, state_high = neighbours(gridpoint_state)
    tallies = encoder_tallies(place, encoder_slots.T, counts, 3 * grid_dev)
    tallies, far_share = tie((tallies, far_share))
    both = jnp.stack([share, far_share])
    ahead, behind = [turn(both, NODE[2], 1)], [turn(both, NODE[2], -1)]
    pooled = pool(tallies, state_low, gridpoint_state, state_high, counts)
    pooled, ahead[0], behind[0] = tie((pooled, ahead[0], behind[0]))
    start, normed = embed(pooled, perturb, embed_weight, norm_gains)
    for _ in range(2):
        ahead.append(turn(ahead[-1], NODE[2], 1))
        behind.append(turn(behind[-1], NODE[2], -1))
    start, normed, ahead[2], behind[2] = tie((start, normed, ahead[2], behind[2]))
    normed_low, normed_high = neighbours(normed)
    ahead.append(turn(ahead[-1], NODE[2], 1))
    column, far = in_order(place, [both] + behind + ahead[::-1])

    before = turn(column, NODE[1], 1)
    after = turn(column, NODE[1], -1)
    other_column = beside(column)
    other_far = across(far)
    normed_low, normed_high, before, after, other_column, other_far = tie(
        (normed_low, normed_high, before, after, other_column, other_far)
    )

    other_before = beside(before)
    other_after = across(after)
    query, kv = qkv(normed_low, normed, normed_high, qkv_weight)
    decoder_near = decoder_tallies(place, decoder_slots.T, 3 * node_dev)
    middle, normed_mid = attention(
        place, query, kv, node_reach[None, :], start, norm_gains, out_weight
    )
    shards = (
        column,
        before,
        after,
        far,
        other_column,
        other_before,
        other_after,
        other_far,
    )

    normed_other = other_core(normed_mid)
    part_mine, part_other = mlp_parts(place, normed_mid, normed_other, shards)
    head_rows = jnp.pad(head_weight.T, ((0, -head_weight.shape[1] % 16), (0, 0)))
    projected = head(middle, part_mine, other_core(part_other), norm_gains, head_rows)

    chip = jnp.stack([projected, other_core(projected)])
    fields = jnp.concatenate([chip, lax.ppermute(chip, MEMBER[0], [(0, 1), (1, 0)])])
    fields_low, fields_high = neighbours(fields)
    gradient = crps(
        decoder_near, gridpoint_state, grid_truth, (fields_low, fields, fields_high)
    )
    return gradient.transpose(1, 0, 2)


def solution(mesh):
    torus = Mesh(
        mesh.devices.reshape(2, 2, 2, 4, 8),
        MEMBER + NODE,
    )
    return jax.shard_map(
        per_device,
        mesh=torus,
        in_specs=(
            P(None, NODE),
            P(None, NODE),
            P(NODE, None),
            P(NODE),
            P(NODE),
            P(NODE, None),
            P(MEMBER, NODE, None),
            P(),
            P(),
            P(),
            P(),
            P(NODE, None),
            P(NODE, None),
            P(),
        ),
        out_specs=P(MEMBER, None, NODE),
        check_vma=False,
    )
```

```python
import jax
import jax.numpy as jnp
from jax import lax
from jax.experimental import pallas as pl
from jax.experimental.pallas import tpu as pltpu
from jax.sharding import Mesh
from jax.sharding import PartitionSpec as P

HEADS = 16
HEAD_DIM = 64
BAND = 256
NODE = ("node_0", "node_1", "node_2")
MEMBER = ("member_hi", "member_core")

EPS = 1e-05
SMOOTH = 0.25

F32 = jnp.float32
BF16 = jnp.bfloat16
LANES_BOTH = (((1,), (1,)), ((), ()))


def params(mib):
    return pltpu.CompilerParams(vmem_limit_bytes=mib * 1024 * 1024)


SHORT = pl.CostEstimate(flops=1, bytes_accessed=1, transcendentals=0)


def layer_norm(entries, scale_gain):
    average = jnp.mean(entries, axis=-1, keepdims=True)
    centred = entries - average
    variance = jnp.mean(centred * centred, axis=-1, keepdims=True)
    return centred * lax.rsqrt(variance + EPS) * scale_gain


def score_gradient(difference):
    return difference * lax.rsqrt(difference * difference + SMOOTH * SMOOTH)


def dot(left_side, right_side):
    return jnp.dot(left_side, right_side, preferred_element_type=F32)


def dot_lanes(left_side, right_side):
    return lax.dot_general(left_side, right_side, LANES_BOTH, preferred_element_type=F32)


def neighbours(block):
    count = lax.axis_size(NODE)
    forward = [(i, (i + 1) % count) for i in range(count)]
    backward = [(target, source) for source, target in forward]
    return lax.ppermute(block, NODE, forward), lax.ppermute(block, NODE, backward)


def other_core(block):
    return lax.ppermute(block, "member_core", [(0, 1), (1, 0)])


def tally_kernel(place_ref, slots_ref, count_ref, out_ref):
    nodes = out_ref.shape[1]
    tall, rows = 256, 64
    slots = slots_ref[...] - place_ref[2]
    used = lax.broadcasted_iota(jnp.int32, slots.shape, 0) < count_ref[...]
    slots = jnp.where(used, slots, -1)
    high = slots >> 8
    low = (slots & 255).astype(F32)
    window = lax.broadcasted_iota(jnp.int32, (tall, nodes), 0).astype(F32).astype(BF16)
    one, zero = jnp.ones((), BF16), jnp.zeros((), BF16)

    def body(step, carry):
        first = pl.multiple_of(step * tall, tall)
        keys = jnp.where(high == step, low, -1.0).astype(BF16)
        for start in range(0, tall, rows):
            total = jnp.zeros((rows, nodes), BF16)
            for position in range(slots.shape[0]):
                hit = keys[position : position + 1, :] == window[start : start + rows, :]
                total = total + jnp.where(hit, one, zero)
            out_ref[pl.ds(first + start, rows), :] = total
        return carry

    lax.fori_loop(0, out_ref.shape[0] // tall, body, 0)


def encoder_tallies(place, slots, counts, width):
    count, nodes = slots.shape
    vmem = pl.BlockSpec(memory_space=pltpu.VMEM)
    return pl.pallas_call(
        tally_kernel,
        out_shape=jax.ShapeDtypeStruct((width, nodes), BF16),
        in_specs=[pl.BlockSpec(memory_space=pltpu.SMEM), vmem, vmem],
        compiler_params=params(16),
        cost_estimate=SHORT,
        name="encoder_tallies",
    )(place, slots, counts)


def pooled_kernel(tally_ref, low_ref, own_ref, high_ref, count_ref, out_ref):
    width = low_ref.shape[1]
    total = dot(own_ref[...], tally_ref[width : 2 * width, :])
    total = total + dot(low_ref[...], tally_ref[:width, :])
    total = total + dot(high_ref[...], tally_ref[2 * width :, :])
    out_ref[...] = (total / count_ref[...].astype(F32)).astype(BF16)


def pool(tallies, low, own, high, counts):
    nodes = tallies.shape[1]
    channels = own.shape[0]
    return pl.pallas_call(
        pooled_kernel,
        out_shape=jax.ShapeDtypeStruct((channels, nodes), BF16),
        compiler_params=params(24),
        cost_estimate=SHORT,
        name="pooled",
    )(tallies, low, own, high, counts)


def embed_kernel(pooled_ref, perturb_ref, embed_ref, gain_ref, start_ref, normed_ref):
    embedded = lax.dot_general(
        pooled_ref[...], embed_ref[...], (((0,), (0,)), ((), ())), preferred_element_type=F32
    )
    start = embedded + perturb_ref[...].astype(F32)
    start_ref[...] = start
    normed_ref[...] = layer_norm(start, gain_ref[0:1, :]).astype(BF16)


def embed(pooled, perturb, embed_weight, norm_gains):
    return pl.pallas_call(
        embed_kernel,
        out_shape=(
            jax.ShapeDtypeStruct(perturb.shape, F32),
            jax.ShapeDtypeStruct(perturb.shape, BF16),
        ),
        compiler_params=params(16),
        cost_estimate=SHORT,
        name="embed",
    )(pooled, perturb, embed_weight, norm_gains)


def qkv_kernel(low_ref, own_ref, high_ref, qkv_hbm, query_ref, kv_ref, qkv_ref, sem):
    copy = pltpu.make_async_copy(qkv_hbm, qkv_ref, sem)
    copy.start()
    nodes, width = own_ref.shape
    copy.wait()
    query = dot(own_ref[...], qkv_ref[:, :width]).astype(BF16)
    query_ref[...] = query * jnp.asarray(HEAD_DIM ** (-0.5), BF16)
    for place, normed in enumerate((low_ref, own_ref, high_ref)):
        for half in range(2):
            columns = slice((half + 1) * width, (half + 2) * width)
            kv_ref[place * nodes : (place + 1) * nodes, half * width : (half + 1) * width] = dot(
                normed[...], qkv_ref[:, columns]
            ).astype(BF16)


def qkv(low, own, high, qkv_weight):
    nodes, width = own.shape
    vmem = pl.BlockSpec(memory_space=pltpu.VMEM)
    return pl.pallas_call(
        qkv_kernel,
        out_shape=(
            jax.ShapeDtypeStruct((nodes, width), BF16),
            jax.ShapeDtypeStruct((3 * nodes, 2 * width), BF16),
        ),
        in_specs=[vmem] * 3 + [pl.BlockSpec(memory_space=pl.ANY)],
        scratch_shapes=[pltpu.VMEM(qkv_weight.shape, BF16), pltpu.SemaphoreType.DMA],
        compiler_params=params(32),
        cost_estimate=SHORT,
        name="qkv",
    )(low, own, high, qkv_weight)


def attention_kernel(
    where_ref, query_ref, kv_ref, reach_ref, attended_ref, cap_ref,
):
    nodes, width = query_ref.shape
    rows = cap_ref.shape[1]
    span = cap_ref.shape[2]
    first_query = where_ref[0]
    node_total = where_ref[1]
    reaches = jnp.transpose(jnp.broadcast_to(reach_ref[...].astype(F32), (128, nodes)))
    for block in range(nodes // rows):
        at = first_query + block * rows + lax.broadcasted_iota(jnp.int32, (rows, span), 0)
        key = first_query - BAND + block * rows + lax.broadcasted_iota(jnp.int32, (rows, span), 1)
        reach = reaches[block * rows : (block + 1) * rows, :1].astype(jnp.int32)
        allowed = (jnp.abs(at - key) <= reach) & (key >= 0) & (key < node_total)
        cap_ref[block] = jnp.where(allowed, 3e38, -1e30)

    lane = lax.broadcasted_iota(jnp.int32, (1, 2 * HEAD_DIM), 1)
    for block in range(nodes // rows):
        cap = cap_ref.at[block]
        for pair in range(HEADS // 2):
            columns = slice(pair * 2 * HEAD_DIM, (pair + 1) * 2 * HEAD_DIM)
            value_columns = slice(width + pair * 2 * HEAD_DIM, width + (pair + 1) * 2 * HEAD_DIM)
            queries = query_ref[block * rows : (block + 1) * rows, columns]
            keys = kv_ref[block * rows : block * rows + span, columns]
            values = kv_ref[block * rows : block * rows + span, value_columns]
            nothing = jnp.zeros_like(queries)
            chosen = jnp.concatenate(
                [
                    jnp.where(lane < HEAD_DIM, queries, nothing),
                    jnp.where(lane < HEAD_DIM, nothing, queries),
                ],
                axis=0,
            )
            scores = dot_lanes(chosen, keys)
            scores = jnp.minimum(scores.reshape(2, rows, span), cap[...][None])
            highest = jnp.max(scores, axis=-1, keepdims=True)
            weights = jnp.exp(scores - highest)
            total = jnp.sum(weights, axis=-1, keepdims=True)
            blended = dot(weights.astype(BF16).reshape(2 * rows, span), values)
            blended = blended.reshape(2, rows, 2 * HEAD_DIM) * (1.0 / total)
            attended_ref[block * rows : (block + 1) * rows, columns] = jnp.where(
                lane < HEAD_DIM, blended[0], blended[1]
            ).astype(BF16)


def middle_kernel(start_ref, attended_ref, out_ref, gain_ref, mid_ref, normed_ref):
    middle = start_ref[...] + dot(attended_ref[...], out_ref[...])
    mid_ref[...] = middle
    normed_ref[...] = layer_norm(middle, gain_ref[1:2, :]).astype(BF16)


def middle_of(start, attended, out_weight, norm_gains):
    return pl.pallas_call(
        middle_kernel,
        out_shape=(
            jax.ShapeDtypeStruct(start.shape, F32),
            jax.ShapeDtypeStruct(start.shape, BF16),
        ),
        compiler_params=params(24),
        cost_estimate=SHORT,
        name="middle",
    )(start, attended, out_weight, norm_gains)


def attention(where, query, kv, reach):
    nodes, width = query.shape
    rows = 128
    span = rows + 2 * BAND
    vmem = pl.BlockSpec(memory_space=pltpu.VMEM)
    return pl.pallas_call(
        attention_kernel,
        out_shape=jax.ShapeDtypeStruct((nodes, width), BF16),
        in_specs=[pl.BlockSpec(memory_space=pltpu.SMEM)] + [vmem] * 3,
        scratch_shapes=[pltpu.VMEM((nodes // rows, rows, span), F32)],
        compiler_params=params(32),
        cost_estimate=SHORT,
        name="attention",
    )(where, query, kv, reach)


def in_order_kernel(place_ref, *refs):
    count = len(refs) - 2
    for shift in range(count):
        at = lax.rem(place_ref[4] + shift, count)
        for side in range(2):
            refs[count + side][at] = refs[shift][side]


def in_order(place, blocks):
    count = len(blocks)
    vmem = pl.BlockSpec(memory_space=pltpu.VMEM)
    return pl.pallas_call(
        in_order_kernel,
        out_shape=(jax.ShapeDtypeStruct((count,) + blocks[0].shape[1:], BF16),) * 2,
        in_specs=[pl.BlockSpec(memory_space=pltpu.SMEM)] + [vmem] * count,
        compiler_params=params(24),
        cost_estimate=SHORT,
        name="shards_in_order",
    )(place, *blocks)


def mlp_kernel(place_ref, own_ref, other_ref, *refs):
    blocks = refs[:-4]
    own_out, other_out, tokens_ref, total_ref = refs[-4:]
    nodes, width = own_ref.shape
    part = width // 8
    hidden = blocks[0].shape[2]
    rows = blocks[0].shape[1] // 2
    step = 512

    def at(block):
        along_x = lax.rem(place_ref[3] + (0, 3, 1, 2)[block % 4], 4)
        along_y = place_ref[5] if block < 4 else 1 - place_ref[5]
        return pl.ds(pl.multiple_of((along_y * 4 + along_x) * part, part), part)

    for block in range(8):
        columns = slice(block * part, (block + 1) * part)
        tokens_ref[:nodes, columns] = other_ref[:, at(block)]
        tokens_ref[nodes:, columns] = own_ref[:, at(block)]

    def all_rows(first, chosen):
        pieces = []
        for block in blocks:
            piece = block[:, first : first + rows, chosen]
            pieces.append(piece.reshape(piece.shape[0] * rows, step))
        return jnp.concatenate(pieces, axis=0)

    for start in range(0, hidden, step):
        chosen = slice(start, start + step)
        upper = dot(tokens_ref[...], all_rows(0, chosen))
        active = jax.nn.gelu(upper).astype(BF16)
        lowered = dot_lanes(active, all_rows(rows, chosen))
        if start == 0:
            total_ref[...] = lowered
        else:
            total_ref[...] += lowered
    for block in range(8):
        columns = slice(block * part, (block + 1) * part)
        other_out[:, at(block)] = total_ref[:nodes, columns].astype(BF16)
        own_out[:, at(block)] = total_ref[nodes:, columns]


def mlp_parts(place, own, other, blocks):
    nodes, width = own.shape
    hidden = blocks[0].shape[2]
    vmem = pl.BlockSpec(memory_space=pltpu.VMEM)
    return pl.pallas_call(
        mlp_kernel,
        out_shape=(
            jax.ShapeDtypeStruct((nodes, width), F32),
            jax.ShapeDtypeStruct((nodes, width), BF16),
        ),
        in_specs=[pl.BlockSpec(memory_space=pltpu.SMEM)] + [vmem] * (2 + len(blocks)),
        scratch_shapes=[
            pltpu.VMEM((2 * nodes, width), BF16),
            pltpu.VMEM((2 * nodes, width), F32),
        ],
        compiler_params=params(40),
        cost_estimate=SHORT,
        name="mlp_parts",
    )(place, own, other, *blocks)


def turn(block, axis, step):
    count = lax.axis_size(axis)
    return lax.ppermute(block, axis, [(i, (i + step) % count) for i in range(count)])


def beside(block):
    return lax.ppermute(block, NODE[0], [(0, 1), (1, 0)])


def across(block):
    return lax.ppermute(block, (MEMBER[0], NODE[0]), [(0, 3), (3, 0), (1, 2), (2, 1)])


def head_kernel(mid_ref, own_ref, other_ref, gain_ref, head_ref, out_ref):
    ending = mid_ref[...] + (own_ref[...] + other_ref[...].astype(F32))
    final = layer_norm(ending, gain_ref[2:3, :]).astype(BF16)
    out_ref[...] = dot_lanes(head_ref[...], final).astype(BF16)


def head(middle, own, other, norm_gains, head_rows):
    nodes, width = middle.shape
    variables = head_rows.shape[0]
    return pl.pallas_call(
        head_kernel,
        out_shape=jax.ShapeDtypeStruct((variables, nodes), BF16),
        compiler_params=params(24),
        cost_estimate=SHORT,
        name="final_head",
    )(middle, own, other, norm_gains, head_rows)


def decoder_tally_kernel(place_ref, slots_ref, out_ref):
    rows = 64
    points = out_ref.shape[1]
    slots = slots_ref.shape[0]

    def body(step, carry):
        first = pl.multiple_of(step * rows, rows)
        node = first + place_ref[7] + lax.broadcasted_iota(jnp.int32, (rows, points), 0)
        total = jnp.zeros((rows, points), F32)
        for position in range(slots):
            hit = slots_ref[position : position + 1, :] == node
            total = total + jnp.where(hit, 1.0 / slots, 0.0)
        out_ref[pl.ds(first, rows), :] = total.astype(BF16)
        return carry

    lax.fori_loop(0, out_ref.shape[0] // rows, body, 0)


def decoder_tallies(place, slots, nodes):
    count, points = slots.shape
    return pl.pallas_call(
        decoder_tally_kernel,
        in_specs=[
            pl.BlockSpec(memory_space=pltpu.SMEM),
            pl.BlockSpec(memory_space=pltpu.VMEM),
        ],
        out_shape=jax.ShapeDtypeStruct((nodes, points), BF16),
        compiler_params=params(16),
        cost_estimate=SHORT,
        name="decoder_tallies",
    )(place, slots)


def crps_kernel(tally_ref, state_ref, truth_ref, *refs):
    out_ref, forecast_ref = refs[-2:]
    field_refs = refs[:-2]
    per_ref, padded, nodes = field_refs[0].shape
    variables = truth_ref.shape[0]
    state = state_ref[:variables, :].astype(F32)
    members = 0
    for first in range(0, len(field_refs), 3):
        delta = None
        for at in range(3):
            stacked = field_refs[first + at][...].reshape(per_ref * padded, nodes)
            term = dot(stacked, tally_ref[at * nodes : (at + 1) * nodes, :])
            delta = term if delta is None else delta + term
        for k in range(per_ref):
            forecast_ref[members] = state + delta[k * padded : k * padded + variables]
            members += 1
    own = forecast_ref[0]
    pairwise = None
    for member in range(members):
        term = score_gradient(own - forecast_ref[member])
        pairwise = term if pairwise is None else pairwise + term
    gradient = score_gradient(own - truth_ref[...].astype(F32)) * (1.0 / members) - pairwise * (
        1.0 / (members * (members - 1))
    )
    out_ref[...] = gradient[:, None, :]


def crps(tallies, state, truth, fields):
    variables, points = truth.shape
    members = len(fields) // 3 * fields[0].shape[0]
    return pl.pallas_call(
        crps_kernel,
        out_shape=jax.ShapeDtypeStruct((variables, 1, points), F32),
        scratch_shapes=[pltpu.VMEM((members, variables, points), F32)],
        compiler_params=params(32),
        cost_estimate=SHORT,
        name="decoder_crps",
    )(tallies, state, truth, *fields)


def per_device(
    gridpoint_state,
    grid_truth,
    encoder_slots,
    encoder_count,
    node_reach,
    decoder_slots,
    member_perturb,
    embed_weight,
    norm_gains,
    qkv_weight,
    out_weight,
    up_weight,
    down_weight,
    head_weight,
):
    region = lax.axis_index(NODE)
    region_count = lax.axis_size(NODE)
    core = lax.axis_index("member_core")
    grid_dev = gridpoint_state.shape[1]
    node_dev = encoder_slots.shape[0]
    hidden = up_weight.shape[1] // 2
    perturb = member_perturb[0]

    place = jnp.stack(
        [
            region * node_dev,
            region_count * node_dev,
            (region - 1) * grid_dev,
            lax.axis_index(NODE[1]),
            lax.axis_index(NODE[2]),
            lax.axis_index(NODE[0]),
            lax.axis_index(MEMBER),
            (region - 1) * node_dev,
        ]
    ).astype(jnp.int32)

    share = jnp.concatenate(
        [
            lax.dynamic_slice_in_dim(up_weight, core * hidden, hidden, 1),
            lax.dynamic_slice_in_dim(down_weight, core * hidden, hidden, 1),
        ],
        axis=0,
    )
    counts = encoder_count[None, :]
    tie = lax.optimization_barrier

    far_share = turn(share, NODE[1], 2)
    state_low, state_high = neighbours(gridpoint_state)
    tallies = encoder_tallies(place, encoder_slots.T, counts, 3 * grid_dev)
    tallies, far_share = tie((tallies, far_share))
    both = jnp.stack([share, far_share])
    ahead, behind = [turn(both, NODE[2], 1)], [turn(both, NODE[2], -1)]
    pooled = pool(tallies, state_low, gridpoint_state, state_high, counts)
    pooled, ahead[0], behind[0] = tie((pooled, ahead[0], behind[0]))
    start, normed = embed(pooled, perturb, embed_weight, norm_gains)
    for _ in range(2):
        ahead.append(turn(ahead[-1], NODE[2], 1))
        behind.append(turn(behind[-1], NODE[2], -1))
    start, normed, ahead[2], behind[2] = tie((start, normed, ahead[2], behind[2]))
    normed_low, normed_high = neighbours(normed)
    ahead.append(turn(ahead[-1], NODE[2], 1))
    column, far = in_order(place, [both] + behind + ahead[::-1])

    before = turn(column, NODE[1], 1)
    after = turn(column, NODE[1], -1)
    other_column = beside(column)
    other_far = across(far)
    query, kv = qkv(normed_low, normed, normed_high, qkv_weight)
    decoder_near = decoder_tallies(place, decoder_slots.T, 3 * node_dev)
    query, kv, decoder_near, before, after, other_column, other_far = tie(
        (query, kv, decoder_near, before, after, other_column, other_far)
    )

    half = column.shape[0] // 2
    other_before = (beside(before[:half]), turn(other_column[half:], NODE[1], 1))
    other_after = (across(after[:half]), turn(other_column[half:], NODE[1], -1))
    attended = attention(place, query, kv, node_reach[None, :])
    attended, other_before, other_after = tie((attended, other_before, other_after))
    middle, normed_mid = middle_of(start, attended, out_weight, norm_gains)
    shards = (
        column,
        before,
        after,
        far,
        other_column,
        *other_before,
        *other_after,
        other_far,
    )

    normed_other = other_core(normed_mid)
    part_mine, part_other = mlp_parts(place, normed_mid, normed_other, shards)
    head_rows = jnp.pad(head_weight.T, ((0, -head_weight.shape[1] % 16), (0, 0)))
    projected = head(middle, part_mine, other_core(part_other), norm_gains, head_rows)

    chip = jnp.stack([projected, other_core(projected)])
    fields = jnp.concatenate([chip, lax.ppermute(chip, MEMBER[0], [(0, 1), (1, 0)])])
    fields_low, fields_high = neighbours(fields)
    gradient = crps(
        decoder_near, gridpoint_state, grid_truth, (fields_low, fields, fields_high)
    )
    return gradient.transpose(1, 0, 2)


def solution(mesh):
    torus = Mesh(
        mesh.devices.reshape(2, 2, 2, 4, 8),
        MEMBER + NODE,
    )
    return jax.shard_map(
        per_device,
        mesh=torus,
        in_specs=(
            P(None, NODE),
            P(None, NODE),
            P(NODE, None),
            P(NODE),
            P(NODE),
            P(NODE, None),
            P(MEMBER, NODE, None),
            P(),
            P(),
            P(),
            P(),
            P(NODE, None),
            P(NODE, None),
            P(),
        ),
        out_specs=P(MEMBER, None, NODE),
        check_vma=False,
    )
```

```python
import jax
import jax.numpy as jnp
from jax import lax
from jax.experimental import pallas as pl
from jax.experimental.pallas import tpu as pltpu
from jax.sharding import Mesh
from jax.sharding import PartitionSpec as P

HEADS = 16
HEAD_DIM = 64
BAND = 256
NODE = ("node_0", "node_1", "node_2")
MEMBER = ("member_hi", "member_core")

EPS = 1e-05
SMOOTH = 0.25

F32 = jnp.float32
BF16 = jnp.bfloat16
LANES_BOTH = (((1,), (1,)), ((), ()))


def params(mib):
    return pltpu.CompilerParams(vmem_limit_bytes=mib * 1024 * 1024)


SHORT = pl.CostEstimate(flops=1, bytes_accessed=1, transcendentals=0)


def layer_norm(entries, scale_gain):
    average = jnp.mean(entries, axis=-1, keepdims=True)
    centred = entries - average
    variance = jnp.mean(centred * centred, axis=-1, keepdims=True)
    return centred * lax.rsqrt(variance + EPS) * scale_gain


def score_gradient(difference):
    return difference * lax.rsqrt(difference * difference + SMOOTH * SMOOTH)


def dot(left_side, right_side):
    return jnp.dot(left_side, right_side, preferred_element_type=F32)


def dot_lanes(left_side, right_side):
    return lax.dot_general(left_side, right_side, LANES_BOTH, preferred_element_type=F32)


def neighbours(block):
    count = lax.axis_size(NODE)
    forward = [(i, (i + 1) % count) for i in range(count)]
    backward = [(target, source) for source, target in forward]
    return lax.ppermute(block, NODE, forward), lax.ppermute(block, NODE, backward)


def other_core(block):
    return lax.ppermute(block, "member_core", [(0, 1), (1, 0)])


def tally_kernel(place_ref, slots_ref, count_ref, out_ref):
    nodes = out_ref.shape[1]
    tall, rows = 256, 64
    slots = slots_ref[...] - place_ref[2]
    used = lax.broadcasted_iota(jnp.int32, slots.shape, 0) < count_ref[...]
    slots = jnp.where(used, slots, -1)
    high = slots >> 8
    low = (slots & 255).astype(F32)
    window = lax.broadcasted_iota(jnp.int32, (tall, nodes), 0).astype(F32).astype(BF16)
    one, zero = jnp.ones((), BF16), jnp.zeros((), BF16)

    def body(step, carry):
        first = pl.multiple_of(step * tall, tall)
        keys = jnp.where(high == step, low, -1.0).astype(BF16)
        for start in range(0, tall, rows):
            total = jnp.zeros((rows, nodes), BF16)
            for position in range(slots.shape[0]):
                hit = keys[position : position + 1, :] == window[start : start + rows, :]
                total = total + jnp.where(hit, one, zero)
            out_ref[pl.ds(first + start, rows), :] = total
        return carry

    lax.fori_loop(0, out_ref.shape[0] // tall, body, 0)


def encoder_tallies(place, slots, counts, width):
    count, nodes = slots.shape
    vmem = pl.BlockSpec(memory_space=pltpu.VMEM)
    return pl.pallas_call(
        tally_kernel,
        out_shape=jax.ShapeDtypeStruct((width, nodes), BF16),
        in_specs=[pl.BlockSpec(memory_space=pltpu.SMEM), vmem, vmem],
        compiler_params=params(16),
        cost_estimate=SHORT,
        name="encoder_tallies",
    )(place, slots, counts)


def pooled_kernel(
    place_ref, tally_ref, own_ref, low_mine, low_other, high_mine, high_other, count_ref, out_ref
):
    width = own_ref.shape[1]
    part = low_mine.shape[1]
    mine = place_ref[6] * part
    other = part - mine
    total = dot(own_ref[...], tally_ref[width : 2 * width, :])
    for first, held, side in (
        (0, low_mine, mine),
        (0, low_other, other),
        (2 * width, high_mine, mine),
        (2 * width, high_other, other),
    ):
        rows = pl.ds(pl.multiple_of(first + side, part), part)
        total = total + dot(held[...], tally_ref[rows, :])
    out_ref[...] = (total / count_ref[...].astype(F32)).astype(BF16)


def pool(place, tallies, own, near, counts):
    nodes = tallies.shape[1]
    channels = own.shape[0]
    vmem = pl.BlockSpec(memory_space=pltpu.VMEM)
    return pl.pallas_call(
        pooled_kernel,
        out_shape=jax.ShapeDtypeStruct((channels, nodes), BF16),
        in_specs=[pl.BlockSpec(memory_space=pltpu.SMEM)] + [vmem] * 7,
        compiler_params=params(24),
        cost_estimate=SHORT,
        name="pooled",
    )(place, tallies, own, *near, counts)


def embed_kernel(pooled_ref, perturb_ref, embed_ref, gain_ref, start_ref, normed_ref):
    embedded = lax.dot_general(
        pooled_ref[...], embed_ref[...], (((0,), (0,)), ((), ())), preferred_element_type=F32
    )
    start = embedded + perturb_ref[...].astype(F32)
    start_ref[...] = start
    normed_ref[...] = layer_norm(start, gain_ref[0:1, :]).astype(BF16)


def embed(pooled, perturb, embed_weight, norm_gains):
    return pl.pallas_call(
        embed_kernel,
        out_shape=(
            jax.ShapeDtypeStruct(perturb.shape, F32),
            jax.ShapeDtypeStruct(perturb.shape, BF16),
        ),
        compiler_params=params(16),
        cost_estimate=SHORT,
        name="embed",
    )(pooled, perturb, embed_weight, norm_gains)


def qkv_kernel(low_ref, own_ref, high_ref, qkv_hbm, query_ref, kv_ref, qkv_ref, sem):
    copy = pltpu.make_async_copy(qkv_hbm, qkv_ref, sem)
    copy.start()
    nodes, width = own_ref.shape
    copy.wait()
    query = dot(own_ref[...], qkv_ref[:, :width]).astype(BF16)
    query_ref[...] = query * jnp.asarray(HEAD_DIM ** (-0.5), BF16)
    for place, normed in enumerate((low_ref, own_ref, high_ref)):
        for half in range(2):
            columns = slice((half + 1) * width, (half + 2) * width)
            kv_ref[place * nodes : (place + 1) * nodes, half * width : (half + 1) * width] = dot(
                normed[...], qkv_ref[:, columns]
            ).astype(BF16)


def qkv(low, own, high, qkv_weight):
    nodes, width = own.shape
    vmem = pl.BlockSpec(memory_space=pltpu.VMEM)
    return pl.pallas_call(
        qkv_kernel,
        out_shape=(
            jax.ShapeDtypeStruct((nodes, width), BF16),
            jax.ShapeDtypeStruct((3 * nodes, 2 * width), BF16),
        ),
        in_specs=[vmem] * 3 + [pl.BlockSpec(memory_space=pl.ANY)],
        scratch_shapes=[pltpu.VMEM(qkv_weight.shape, BF16), pltpu.SemaphoreType.DMA],
        compiler_params=params(32),
        cost_estimate=SHORT,
        name="qkv",
    )(low, own, high, qkv_weight)


def attention_kernel(
    where_ref, query_ref, kv_ref, reach_ref, attended_ref, cap_ref,
):
    nodes, width = query_ref.shape
    rows = cap_ref.shape[1]
    span = cap_ref.shape[2]
    first_query = where_ref[0]
    node_total = where_ref[1]
    reaches = jnp.transpose(jnp.broadcast_to(reach_ref[...].astype(F32), (128, nodes)))
    for block in range(nodes // rows):
        at = first_query + block * rows + lax.broadcasted_iota(jnp.int32, (rows, span), 0)
        key = first_query - BAND + block * rows + lax.broadcasted_iota(jnp.int32, (rows, span), 1)
        reach = reaches[block * rows : (block + 1) * rows, :1].astype(jnp.int32)
        allowed = (jnp.abs(at - key) <= reach) & (key >= 0) & (key < node_total)
        cap_ref[block] = jnp.where(allowed, 3e38, -1e30)

    lane = lax.broadcasted_iota(jnp.int32, (1, 2 * HEAD_DIM), 1)
    for block in range(nodes // rows):
        cap = cap_ref.at[block]
        for pair in range(HEADS // 2):
            columns = slice(pair * 2 * HEAD_DIM, (pair + 1) * 2 * HEAD_DIM)
            value_columns = slice(width + pair * 2 * HEAD_DIM, width + (pair + 1) * 2 * HEAD_DIM)
            queries = query_ref[block * rows : (block + 1) * rows, columns]
            keys = kv_ref[block * rows : block * rows + span, columns]
            values = kv_ref[block * rows : block * rows + span, value_columns]
            nothing = jnp.zeros_like(queries)
            chosen = jnp.concatenate(
                [
                    jnp.where(lane < HEAD_DIM, queries, nothing),
                    jnp.where(lane < HEAD_DIM, nothing, queries),
                ],
                axis=0,
            )
            scores = dot_lanes(chosen, keys)
            scores = jnp.minimum(scores.reshape(2, rows, span), cap[...][None])
            highest = jnp.max(scores, axis=-1, keepdims=True)
            weights = jnp.exp(scores - highest)
            total = jnp.sum(weights, axis=-1, keepdims=True)
            blended = dot(weights.astype(BF16).reshape(2 * rows, span), values)
            blended = blended.reshape(2, rows, 2 * HEAD_DIM) * (1.0 / total)
            attended_ref[block * rows : (block + 1) * rows, columns] = jnp.where(
                lane < HEAD_DIM, blended[0], blended[1]
            ).astype(BF16)


def middle_kernel(start_ref, attended_ref, out_ref, gain_ref, mid_ref, normed_ref):
    middle = start_ref[...] + dot(attended_ref[...], out_ref[...])
    mid_ref[...] = middle
    normed_ref[...] = layer_norm(middle, gain_ref[1:2, :]).astype(BF16)


def middle_of(start, attended, out_weight, norm_gains):
    return pl.pallas_call(
        middle_kernel,
        out_shape=(
            jax.ShapeDtypeStruct(start.shape, F32),
            jax.ShapeDtypeStruct(start.shape, BF16),
        ),
        compiler_params=params(24),
        cost_estimate=SHORT,
        name="middle",
    )(start, attended, out_weight, norm_gains)


def attention(where, query, kv, reach):
    nodes, width = query.shape
    rows = 128
    span = rows + 2 * BAND
    vmem = pl.BlockSpec(memory_space=pltpu.VMEM)
    return pl.pallas_call(
        attention_kernel,
        out_shape=jax.ShapeDtypeStruct((nodes, width), BF16),
        in_specs=[pl.BlockSpec(memory_space=pltpu.SMEM)] + [vmem] * 3,
        scratch_shapes=[pltpu.VMEM((nodes // rows, rows, span), F32)],
        compiler_params=params(32),
        cost_estimate=SHORT,
        name="attention",
    )(where, query, kv, reach)


def in_order_kernel(place_ref, *refs):
    count = len(refs) - 2
    for shift in range(count):
        at = lax.rem(place_ref[4] + shift, count)
        for side in range(2):
            refs[count + side][at] = refs[shift][side]


def in_order(place, blocks):
    count = len(blocks)
    vmem = pl.BlockSpec(memory_space=pltpu.VMEM)
    return pl.pallas_call(
        in_order_kernel,
        out_shape=(jax.ShapeDtypeStruct((count,) + blocks[0].shape[1:], BF16),) * 2,
        in_specs=[pl.BlockSpec(memory_space=pltpu.SMEM)] + [vmem] * count,
        compiler_params=params(24),
        cost_estimate=SHORT,
        name="shards_in_order",
    )(place, *blocks)


def mlp_kernel(place_ref, own_ref, other_ref, *refs):
    blocks = refs[:-4]
    own_out, other_out, tokens_ref, total_ref = refs[-4:]
    nodes, width = own_ref.shape
    part = width // 8
    hidden = blocks[0].shape[2]
    rows = blocks[0].shape[1] // 2
    step = 512

    def at(block):
        along_x = lax.rem(place_ref[3] + (0, 3, 1, 2)[block % 4], 4)
        along_y = place_ref[5] if block < 4 else 1 - place_ref[5]
        return pl.ds(pl.multiple_of((along_y * 4 + along_x) * part, part), part)

    for block in range(8):
        columns = slice(block * part, (block + 1) * part)
        tokens_ref[:nodes, columns] = other_ref[:, at(block)]
        tokens_ref[nodes:, columns] = own_ref[:, at(block)]

    def all_rows(first, chosen):
        pieces = []
        for block in blocks:
            piece = block[:, first : first + rows, chosen]
            pieces.append(piece.reshape(piece.shape[0] * rows, step))
        return jnp.concatenate(pieces, axis=0)

    for start in range(0, hidden, step):
        chosen = slice(start, start + step)
        upper = dot(tokens_ref[...], all_rows(0, chosen))
        active = jax.nn.gelu(upper).astype(BF16)
        lowered = dot_lanes(active, all_rows(rows, chosen))
        if start == 0:
            total_ref[...] = lowered
        else:
            total_ref[...] += lowered
    for block in range(8):
        columns = slice(block * part, (block + 1) * part)
        other_out[:, at(block)] = total_ref[:nodes, columns].astype(BF16)
        own_out[:, at(block)] = total_ref[nodes:, columns]


def mlp_parts(place, own, other, blocks):
    nodes, width = own.shape
    hidden = blocks[0].shape[2]
    vmem = pl.BlockSpec(memory_space=pltpu.VMEM)
    return pl.pallas_call(
        mlp_kernel,
        out_shape=(
            jax.ShapeDtypeStruct((nodes, width), F32),
            jax.ShapeDtypeStruct((nodes, width), BF16),
        ),
        in_specs=[pl.BlockSpec(memory_space=pltpu.SMEM)] + [vmem] * (2 + len(blocks)),
        scratch_shapes=[
            pltpu.VMEM((2 * nodes, width), BF16),
            pltpu.VMEM((2 * nodes, width), F32),
        ],
        compiler_params=params(40),
        cost_estimate=SHORT,
        name="mlp_parts",
    )(place, own, other, *blocks)


def turn(block, axis, step):
    count = lax.axis_size(axis)
    return lax.ppermute(block, axis, [(i, (i + step) % count) for i in range(count)])


def beside(block):
    return lax.ppermute(block, NODE[0], [(0, 1), (1, 0)])


def across(block):
    return lax.ppermute(block, (MEMBER[0], NODE[0]), [(0, 3), (3, 0), (1, 2), (2, 1)])


def head_kernel(mid_ref, own_ref, other_ref, gain_ref, head_ref, out_ref):
    ending = mid_ref[...] + (own_ref[...] + other_ref[...].astype(F32))
    final = layer_norm(ending, gain_ref[2:3, :]).astype(BF16)
    out_ref[...] = dot_lanes(head_ref[...], final).astype(BF16)


def head(middle, own, other, norm_gains, head_rows):
    nodes, width = middle.shape
    variables = head_rows.shape[0]
    return pl.pallas_call(
        head_kernel,
        out_shape=jax.ShapeDtypeStruct((variables, nodes), BF16),
        compiler_params=params(24),
        cost_estimate=SHORT,
        name="final_head",
    )(middle, own, other, norm_gains, head_rows)


def decoder_tally_kernel(place_ref, slots_ref, out_ref):
    rows = 64
    points = out_ref.shape[1]
    slots = slots_ref.shape[0]

    def body(step, carry):
        first = pl.multiple_of(step * rows, rows)
        node = first + place_ref[7] + lax.broadcasted_iota(jnp.int32, (rows, points), 0)
        total = jnp.zeros((rows, points), F32)
        for position in range(slots):
            hit = slots_ref[position : position + 1, :] == node
            total = total + jnp.where(hit, 1.0 / slots, 0.0)
        out_ref[pl.ds(first, rows), :] = total.astype(BF16)
        return carry

    lax.fori_loop(0, out_ref.shape[0] // rows, body, 0)


def decoder_tallies(place, slots, nodes):
    count, points = slots.shape
    return pl.pallas_call(
        decoder_tally_kernel,
        in_specs=[
            pl.BlockSpec(memory_space=pltpu.SMEM),
            pl.BlockSpec(memory_space=pltpu.VMEM),
        ],
        out_shape=jax.ShapeDtypeStruct((nodes, points), BF16),
        compiler_params=params(16),
        cost_estimate=SHORT,
        name="decoder_tallies",
    )(place, slots)


def crps_kernel(tally_ref, state_ref, truth_ref, *refs):
    out_ref, forecast_ref = refs[-2:]
    field_refs = refs[:-2]
    per_ref, padded, nodes = field_refs[0].shape
    variables = truth_ref.shape[0]
    state = state_ref[:variables, :].astype(F32)
    members = 0
    for first in range(0, len(field_refs), 3):
        delta = None
        for at in range(3):
            stacked = field_refs[first + at][...].reshape(per_ref * padded, nodes)
            term = dot(stacked, tally_ref[at * nodes : (at + 1) * nodes, :])
            delta = term if delta is None else delta + term
        for k in range(per_ref):
            forecast_ref[members] = state + delta[k * padded : k * padded + variables]
            members += 1
    own = forecast_ref[0]
    pairwise = None
    for member in range(members):
        term = score_gradient(own - forecast_ref[member])
        pairwise = term if pairwise is None else pairwise + term
    gradient = score_gradient(own - truth_ref[...].astype(F32)) * (1.0 / members) - pairwise * (
        1.0 / (members * (members - 1))
    )
    out_ref[...] = gradient[:, None, :]


def crps(tallies, state, truth, fields):
    variables, points = truth.shape
    members = len(fields) // 3 * fields[0].shape[0]
    return pl.pallas_call(
        crps_kernel,
        out_shape=jax.ShapeDtypeStruct((variables, 1, points), F32),
        scratch_shapes=[pltpu.VMEM((members, variables, points), F32)],
        compiler_params=params(32),
        cost_estimate=SHORT,
        name="decoder_crps",
    )(tallies, state, truth, *fields)


def per_device(
    gridpoint_state,
    grid_truth,
    encoder_slots,
    encoder_count,
    node_reach,
    decoder_slots,
    member_perturb,
    embed_weight,
    norm_gains,
    qkv_weight,
    out_weight,
    up_weight,
    down_weight,
    head_weight,
):
    region = lax.axis_index(NODE)
    region_count = lax.axis_size(NODE)
    core = lax.axis_index("member_core")
    grid_dev = gridpoint_state.shape[1]
    node_dev = encoder_slots.shape[0]
    hidden = up_weight.shape[1] // 2
    perturb = member_perturb[0]

    place = jnp.stack(
        [
            region * node_dev,
            region_count * node_dev,
            (region - 1) * grid_dev,
            lax.axis_index(NODE[1]),
            lax.axis_index(NODE[2]),
            lax.axis_index(NODE[0]),
            core,
            (region - 1) * node_dev,
        ]
    ).astype(jnp.int32)

    share = jnp.concatenate(
        [
            lax.dynamic_slice_in_dim(up_weight, core * hidden, hidden, 1),
            lax.dynamic_slice_in_dim(down_weight, core * hidden, hidden, 1),
        ],
        axis=0,
    )
    counts = encoder_count[None, :]
    tie = lax.optimization_barrier

    far_share = turn(share, NODE[1], 2)
    part = grid_dev // 2
    state_part = lax.dynamic_slice_in_dim(gridpoint_state, core * part, part, 1)
    state_low, state_high = neighbours(state_part)
    state_near = (state_low, other_core(state_low), state_high, other_core(state_high))
    tallies = encoder_tallies(place, encoder_slots.T, counts, 3 * grid_dev)
    tallies, far_share = tie((tallies, far_share))
    both = jnp.stack([share, far_share])
    ahead, behind = [turn(both, NODE[2], 1)], [turn(both, NODE[2], -1)]
    pooled = pool(place, tallies, gridpoint_state, state_near, counts)
    pooled, ahead[0], behind[0] = tie((pooled, ahead[0], behind[0]))
    start, normed = embed(pooled, perturb, embed_weight, norm_gains)
    for _ in range(2):
        ahead.append(turn(ahead[-1], NODE[2], 1))
        behind.append(turn(behind[-1], NODE[2], -1))
    start, normed, ahead[2], behind[2] = tie((start, normed, ahead[2], behind[2]))
    normed_low, normed_high = neighbours(normed)
    ahead.append(turn(ahead[-1], NODE[2], 1))
    column, far = in_order(place, [both] + behind + ahead[::-1])

    before = turn(column, NODE[1], 1)
    after = turn(column, NODE[1], -1)
    other_column = beside(column)
    other_far = across(far)
    query, kv = qkv(normed_low, normed, normed_high, qkv_weight)
    decoder_near = decoder_tallies(place, decoder_slots.T, 3 * node_dev)
    query, kv, decoder_near, before, after, other_column, other_far = tie(
        (query, kv, decoder_near, before, after, other_column, other_far)
    )

    half = column.shape[0] // 2
    other_before = (beside(before[:half]), turn(other_column[half:], NODE[1], 1))
    other_after = (across(after[:half]), turn(other_column[half:], NODE[1], -1))
    attended = attention(place, query, kv, node_reach[None, :])
    attended, other_before, other_after = tie((attended, other_before, other_after))
    middle, normed_mid = middle_of(start, attended, out_weight, norm_gains)
    shards = (
        column,
        before,
        after,
        far,
        other_column,
        *other_before,
        *other_after,
        other_far,
    )

    normed_other = other_core(normed_mid)
    part_mine, part_other = mlp_parts(place, normed_mid, normed_other, shards)
    head_rows = jnp.pad(head_weight.T, ((0, -head_weight.shape[1] % 16), (0, 0)))
    projected = head(middle, part_mine, other_core(part_other), norm_gains, head_rows)

    chip = jnp.stack([projected, other_core(projected)])
    fields = jnp.concatenate([chip, lax.ppermute(chip, MEMBER[0], [(0, 1), (1, 0)])])
    fields_low, fields_high = neighbours(fields)
    gradient = crps(
        decoder_near, gridpoint_state, grid_truth, (fields_low, fields, fields_high)
    )
    return gradient.transpose(1, 0, 2)


def solution(mesh):
    torus = Mesh(
        mesh.devices.reshape(2, 2, 2, 4, 8),
        MEMBER + NODE,
    )
    return jax.shard_map(
        per_device,
        mesh=torus,
        in_specs=(
            P(None, NODE),
            P(None, NODE),
            P(NODE, None),
            P(NODE),
            P(NODE),
            P(NODE, None),
            P(MEMBER, NODE, None),
            P(),
            P(),
            P(),
            P(),
            P(NODE, None),
            P(NODE, None),
            P(),
        ),
        out_specs=P(MEMBER, None, NODE),
        check_vma=False,
    )
```
